128 devices in a mesh: tok: 4 (over y_hi, core), blk: 32 (over x, z, y_lo).
Axes of the slice: x: 4, y: 4 (y_hi: 2, y_lo: 2; y = y_hi * 2 + y_lo), z: 4, core: 2. Of those that a mesh axis runs over, the one named last changes fastest.
Arguments:
- tokens: bfloat16 [64, 128, 10240], P('blk', None, 'tok'), may hold values from -6 to 6
- cotangent: bfloat16 [64, 128, 10240], P('blk', None, 'tok'), may hold values from -6 to 6
- right_up: bfloat16 [64, 512, 128], P('blk'), may hold values from -0.5 to 0.5
- left_up: bfloat16 [512, 64, 64], P('blk'), may hold values from -0.75 to 0.75
- left_down: bfloat16 [512, 64, 64], P('blk'), may hold values from -0.75 to 0.75
- right_down: bfloat16 [64, 128, 512], P('blk'), may hold values from -0.25 to 0.25
Outputs:
- output: bfloat16 [64, 128, 10240], P('blk', None, 'tok')
- grad_tokens: bfloat16 [64, 128, 10240], P('blk', None, 'tok')
- grad_right_up: float32 [64, 512, 128], P('blk')
- grad_left_up: float32 [512, 64, 64], P('blk')
- grad_left_down: float32 [512, 64, 64], P('blk')
- grad_right_down: float32 [64, 128, 512], P('blk')
The draws below stay inside these ranges and needn't reach their ends.
All inputs are finite; a program needn't handle non-finite values.
Results may differ from the reference program's by a relative error of at most 0.0068.
Values may be sent and summed in bfloat16 or wider, within the bound.
A program may use at most 192 MiB of HBM per device.

```python
import jax
import jax.numpy as jnp
from jax import lax

BW = 128
NA = 64
NC = 512
TOKENS = 10240


def block_scale(own_key, shape, cuts, low, high):
    def one(dim, parts):
        heights = jax.random.uniform(jax.random.fold_in(jax.random.fold_in(own_key, 6), dim), (parts,), jnp.float32, low / len(cuts), high / len(cuts))
        return jnp.repeat(jnp.exp(heights), shape[dim] // parts).reshape((-1,) + (1,) * (len(shape) - dim - 1))

    gain = one(*cuts[0])
    for cut in cuts[1:]:
        gain = gain * one(*cut)
    return gain


def bell_draw(rng, extent, scale, most, shards=(), kind=jnp.bfloat16):
    entries = jax.random.normal(rng, extent, jnp.float32) * scale
    if len(shards) > 0:
        entries = block_scale(rng, extent, shards, -0.22, 0.18) * entries
    return jnp.clip(entries, min=-most, max=most).astype(kind)


def setup_inputs(seed: int = 0) -> dict:
    splits = jax.random.split(jax.random.key(seed), 7)
    return {
        "tokens": bell_draw(splits[0], (NA, BW, TOKENS), 1.0, 6.0, ((0, 32), (2, 4))),
        "cotangent": bell_draw(splits[1], (NA, BW, TOKENS), 1.0, 6.0, ((0, 32), (2, 4))),
        "right_up": bell_draw(splits[2], (NA, NC, BW), BW ** -0.5, 0.5, ((0, 32),)),
        "left_up": bell_draw(splits[3], (NC, NA, NA), NA ** -0.5, 0.75, ((0, 32),)),
        "left_down": bell_draw(splits[4], (NC, NA, NA), NA ** -0.5, 0.75, ((0, 32),)),
        "right_down": bell_draw(splits[5], (NA, BW, NC), NC ** -0.5, 0.25, ((0, 32),)),
    }


def activate(value):
    return jax.nn.gelu(value, approximate=True)

def rounded(value):
    return lax.optimization_barrier(value.astype(jnp.bfloat16)).astype(jnp.float32)

def reference(tokens, cotangent, right_up, left_up, left_down, right_down):
    block = min(TOKENS, 1024)
    count = TOKENS // block

    def split(array):
        return jnp.moveaxis(array.reshape(array.shape[0], array.shape[1], count, block), 2, 0)

    def join(array):
        return jnp.moveaxis(array, 0, 2).reshape(array.shape[1], array.shape[2], TOKENS)
    ru = right_up.astype(jnp.float32)
    lu = left_up.astype(jnp.float32)
    ld = left_down.astype(jnp.float32)
    rd = right_down.astype(jnp.float32)

    def step(carry, pieces):
        inputs, grads_in = pieces
        xin = inputs.astype(jnp.float32)
        dout = grads_in.astype(jnp.float32)
        first = rounded(jnp.einsum('acb,abt->act', ru, xin))
        pre = jnp.einsum('cea,act->cet', lu, first)
        hidden = rounded(activate(pre))
        mixed = rounded(jnp.einsum('cfe,cet->cft', ld, hidden))
        output = jnp.einsum('fbc,cft->fbt', rd, mixed).astype(jnp.bfloat16)
        back_mixed = rounded(jnp.einsum('fbc,fbt->cft', rd, dout))
        sum_rd = jnp.einsum('fbt,cft->fbc', dout, mixed)
        back_hidden = jnp.einsum('cfe,cft->cet', ld, back_mixed)
        sum_ld = jnp.einsum('cft,cet->cfe', back_mixed, hidden)
        back_pre = rounded(jax.vjp(activate, pre)[1](back_hidden)[0])
        back_first = rounded(jnp.einsum('cea,cet->act', lu, back_pre))
        sum_lu = jnp.einsum('cet,act->cea', back_pre, first)
        grad_in = jnp.einsum('acb,act->abt', ru, back_first).astype(jnp.bfloat16)
        sum_ru = jnp.einsum('act,abt->acb', back_first, xin)
        carry = (carry[0] + sum_ru, carry[1] + sum_lu, carry[2] + sum_ld, carry[3] + sum_rd)
        return (carry, (output, grad_in))
    start = (jnp.zeros(right_up.shape, jnp.float32), jnp.zeros(left_up.shape, jnp.float32), jnp.zeros(left_down.shape, jnp.float32), jnp.zeros(right_down.shape, jnp.float32))
    totals, results = lax.scan(step, start, (split(tokens), split(cotangent)))
    factor = float(TOKENS) ** (-0.5)
    return (join(results[0]), join(results[1]), totals[0] * factor, totals[1] * factor, totals[2] * factor, totals[3] * factor)
```

```python
import functools

import jax
import jax.numpy as jnp
from jax import lax
from jax.experimental import pallas as pl
from jax.experimental.pallas import tpu as pltpu
from jax.sharding import PartitionSpec as P

MESH = pl.DeviceIdType.MESH
CHUNK = 512
SPAN = 256
ROOT = 0.7978845608028654
CUBIC = 0.044715


def dot(a, b):
    return jnp.dot(a, b, preferred_element_type=jnp.float32)


def dot_nt(a, b):
    return lax.dot_general(a, b, (((1,), (1,)), ((), ())), preferred_element_type=jnp.float32)


def kernel(
    chunks, owners, x_ref, cot_ref, w1_ref, w1t_ref, w2_ref, w2t_ref, w3_ref, w3t_ref, w4_ref, w4t_ref,
    out_ref, gt_ref, sums_ref,
    send_a, send_b, got_first, got_back, got_mixed, got_last, hidden, slope, back_pre,
    acc_ru, acc_rd, acc_ld, acc_lu, grads, near, own, far,
    send_sem, recv_sem, sum_send, sum_recv,
):
    me = lax.axis_index("blk")
    tok = lax.axis_index("tok")
    core_peer = tok + 1 - 2 * lax.rem(tok, 2)
    far_peer = tok + 2 - 4 * (tok // 2)
    rows = send_a.shape[2]
    half = rows // 2
    count = owners - 1

    barrier = pltpu.get_barrier_semaphore()

    def greet(i, carry):
        pl.semaphore_signal(barrier, inc=1, device_id=(tok, lax.rem(me + i, owners)), device_id_type=MESH)
        return carry

    lax.fori_loop(1, owners, greet, 0)
    pl.semaphore_signal(barrier, inc=1, device_id=(core_peer, me), device_id_type=MESH)
    pl.semaphore_signal(barrier, inc=1, device_id=(far_peer, me), device_id_type=MESH)

    for acc in (acc_ru, acc_rd, acc_ld, acc_lu):
        acc[...] = jnp.zeros_like(acc)

    def columns(k):
        return pl.ds(pl.multiple_of(k * CHUNK, CHUNK), CHUNK)

    def post(kind, k, source, target):
        pltpu.make_async_copy(source.at[k, me], target.at[k, me], recv_sem.at[kind, k]).start()

        def one(i, carry):
            to = lax.rem(me + i, owners)
            pltpu.make_async_remote_copy(
                src_ref=source.at[k, to], dst_ref=target.at[k, me],
                send_sem=send_sem.at[kind, k], recv_sem=recv_sem.at[kind, k],
                device_id=(tok, to), device_id_type=MESH,
            ).start()
            return carry

        lax.fori_loop(1, owners, one, 0)

    def sent(kind, k, source):
        part = source.at[k, pl.ds(0, count)]
        pltpu.make_async_copy(part, part, send_sem.at[kind, k]).wait()

    def arrived(kind, k, target):
        pltpu.make_async_copy(target.at[k], target.at[k], recv_sem.at[kind, k]).wait()

    wide = SPAN // rows

    def spread(w_ref, data, buffer, k):
        def part(r, carry):
            w = w_ref[pl.ds(pl.multiple_of(r * SPAN, SPAN), SPAN), :]
            value = dot(w, data).astype(jnp.bfloat16)
            buffer[k, pl.ds(r * wide, wide)] = value.reshape(wide, rows, CHUNK)
            return carry

        lax.fori_loop(0, w_ref.shape[0] // SPAN, part, 0)

    def stage_first(k):
        spread(w1_ref, x_ref[:, columns(k)], send_a, k)

    def stage_back(k):
        spread(w4t_ref, cot_ref[:, columns(k)], send_b, k)

    def rows_of(buffer, k, h):
        return buffer[k, :, h * half:(h + 1) * half, :].reshape(owners * half, CHUNK)

    def keep_block(acc, h, r, value):
        which = lax.rem(lax.broadcasted_iota(jnp.int32, (SPAN, 128), 0), half) // 4
        kept = value[:, 0:128]
        for p in range(1, half // 4):
            kept = jnp.where(which == p, value[:, p * 128:(p + 1) * 128], kept)
        acc[h, r * SPAN:(r + 1) * SPAN, :] += kept

    def stage_middle(k):
        arrived(0, k, got_first)
        sent(0, k, send_a)
        size = owners * half
        for h in range(2):
            given = rows_of(got_first, k, h)
            for r in range(size // SPAN):
                at = pl.ds(r * SPAN, SPAN)
                pre = dot(w2_ref[h, at, :], given)
                square = pre * pre
                t = jnp.tanh(ROOT * (pre + CUBIC * (square * pre)))
                cdf = 0.5 * (1.0 + t)
                hidden[h, at, :] = (pre * cdf).astype(jnp.bfloat16)
                slope[h, at, :] = cdf + (0.5 * ROOT) * pre * (1.0 - t * t) * (1.0 + (3.0 * CUBIC) * square)
        each = SPAN // half
        for h in range(2):
            for r in range(size // SPAN):
                value = dot(w3_ref[h, pl.ds(r * SPAN, SPAN), :], hidden[h]).astype(jnp.bfloat16)
                send_a[k, r * each:(r + 1) * each, h * half:(h + 1) * half, :] = value.reshape(each, half, CHUNK)
        post(2, k, send_a, got_mixed)

        arrived(1, k, got_back)
        sent(1, k, send_b)
        for h in range(2):
            given = rows_of(got_back, k, h)
            for r in range(size // SPAN):
                at = pl.ds(r * SPAN, SPAN)
                back = dot(w3t_ref[h, at, :], given)
                back_pre[h, at, :] = (back * slope[h, at, :]).astype(jnp.bfloat16)
        for h in range(2):
            for r in range(size // SPAN):
                value = dot(w2t_ref[h, pl.ds(r * SPAN, SPAN), :], back_pre[h]).astype(jnp.bfloat16)
                send_b[k, r * each:(r + 1) * each, h * half:(h + 1) * half, :] = value.reshape(each, half, CHUNK)
        post(3, k, send_b, got_last)

        for h in range(2):
            for r in range(size // SPAN):
                part = slice(r * each, (r + 1) * each)
                inner = slice(h * half, (h + 1) * half)
                back = got_back[k, part, inner, :].reshape(SPAN, CHUNK)
                keep_block(acc_ld, h, r, dot_nt(back, hidden[h]))
                first = got_first[k, part, inner, :].reshape(SPAN, CHUNK)
                keep_block(acc_lu, h, r, dot_nt(first, back_pre[h]))

    def gather(k, got, w_ref, data_ref, into_ref, acc):
        data = data_ref[:, columns(k)]
        everything = got[k].reshape(owners * rows, CHUNK)
        into_ref[:, columns(k)] = dot(w_ref[...], everything).astype(jnp.bfloat16)
        odd = lax.rem(lax.broadcasted_iota(jnp.int32, (SPAN, 128), 0), 2) == 1

        def part(r, carry):
            piece = got[k, pl.ds(r * wide, wide)].reshape(SPAN, CHUNK)
            value = dot_nt(piece, data)
            at = pl.ds(pl.multiple_of(r * SPAN, SPAN), SPAN)
            acc[at, :] += jnp.where(odd, value[:, 128:256], value[:, 0:128])
            return carry

        lax.fori_loop(0, owners * rows // SPAN, part, 0)

    def stage_output(k):
        arrived(2, k, got_mixed)
        gather(k, got_mixed, w4_ref, cot_ref, out_ref, acc_rd)

    def stage_grad(k):
        arrived(3, k, got_last)
        gather(k, got_last, w1t_ref, x_ref, gt_ref, acc_ru)

    stage_first(0)
    stage_back(0)
    pl.semaphore_wait(barrier, count + 2)
    post(0, 0, send_a, got_first)
    post(1, 0, send_b, got_back)

    def ahead(k):
        stage_first(k)
        post(0, k, send_a, got_first)
        stage_back(k)
        post(1, k, send_b, got_back)

    ahead(1)

    def step(k, carry):
        stage_middle(k)

        @pl.when(k + 2 < chunks)
        def _():
            ahead(k + 2)

        @pl.when(k >= 1)
        def _():
            stage_output(k - 1)
            stage_grad(k - 1)

        return carry

    lax.fori_loop(0, chunks, step, 0)

    part = grads.shape[1] // 2
    core = lax.rem(tok, 2)
    mine = pl.ds(pl.multiple_of(core * part, part), part)
    theirs = pl.ds(pl.multiple_of(part - core * part, part), part)

    def pair(i):
        return pltpu.make_async_remote_copy(
            src_ref=grads.at[i, theirs], dst_ref=near.at[i], send_sem=sum_send.at[0, i], recv_sem=sum_recv.at[0, i],
            device_id=(core_peer, me), device_id_type=MESH,
        )

    def across(i):
        return pltpu.make_async_remote_copy(
            src_ref=own.at[i], dst_ref=far.at[i], send_sem=sum_send.at[1, i], recv_sem=sum_recv.at[1, i],
            device_id=(far_peer, me), device_id_type=MESH,
        )

    def share(i):
        return pltpu.make_async_remote_copy(
            src_ref=sums_ref.at[i, mine], dst_ref=sums_ref.at[i, mine],
            send_sem=sum_send.at[2, i], recv_sem=sum_recv.at[2, i],
            device_id=(core_peer, me), device_id_type=MESH,
        )

    def begin(i):
        pair(i).start()

    def middle(i):
        pair(i).wait()
        own[i] = grads[i, mine, :] + near[i]
        across(i).start()

    def finish(i):
        across(i).wait()
        sums_ref[i, mine, :] = own[i] + far[i]
        share(i).start()

    lane = lax.broadcasted_iota(jnp.int32, (owners, 128), 1)
    for h in range(2):
        for c in range(half // 2):
            for s in range(2):
                ld = acc_ld[h, pl.ds(2 * c + s, owners, stride=half), :]
                lu = acc_lu[h, pl.ds(2 * c + s, owners, stride=half), :]
                if c % 2 == 0:
                    both = jnp.where(lane < 64, ld, pltpu.roll(lu, 64, 1))
                else:
                    both = jnp.where(lane < 64, pltpu.roll(ld, 64, 1), lu)
                base = (h * (half // 2) + c) * 2 * owners
                grads[0, pl.ds(base + s, owners, stride=2), :] = both
    begin(0)

    size = owners * half
    last = chunks - 1
    stage_output(last)
    for s in range(2):
        grads[1, s * size:(s + 1) * size, :] = acc_rd[pl.ds(s, size, stride=2), :]
    begin(1)
    middle(0)
    middle(1)
    stage_grad(last)
    for s in range(2):
        grads[2, s * size:(s + 1) * size, :] = acc_ru[pl.ds(s, size, stride=2), :]
    begin(2)
    finish(0)
    finish(1)
    middle(2)
    finish(2)

    def drain(k, carry):
        sent(2, k, send_a)
        sent(3, k, send_b)
        return carry

    lax.fori_loop(0, chunks, drain, 0)
    for i in range(3):
        share(i).wait()


def shards(tokens, cotangent, right_up, left_up, left_down, right_down):
    tok_count = lax.axis_size("tok")
    owners = lax.axis_size("blk")
    factor = float(tokens.shape[2] * tok_count) ** (-0.5)
    pair, width, count = tokens.shape
    hidden_blocks = right_up.shape[1]
    own_blocks = left_up.shape[0]
    units = left_up.shape[1]
    eight = own_blocks // 2
    chunks = count // CHUNK
    bf = jnp.bfloat16

    two = jnp.eye(pair, dtype=bf)
    eye = jnp.eye(eight, dtype=bf)
    wide, deep = pair * hidden_blocks, pair * width
    w1 = (right_up.transpose(1, 0, 2)[:, :, None, :] * two[None, :, :, None]).reshape(wide, deep)
    w1t = (right_up.transpose(0, 2, 1)[:, :, :, None] * two[:, None, None, :]).reshape(deep, wide)
    w4 = (right_down[:, :, :, None] * two[:, None, None, :]).reshape(deep, wide)
    w4t = (right_down.transpose(2, 0, 1)[:, :, None, :] * two[None, :, :, None]).reshape(wide, deep)
    size = eight * units
    up = left_up.reshape(2, eight, units, owners, pair)
    w2 = (up[:, :, :, :, None, :] * eye[None, :, None, None, :, None]).reshape(2, size, size)
    w2t = (up.transpose(0, 3, 1, 4, 2)[:, :, :, :, None, :] * eye[None, None, :, None, :, None]).reshape(2, size, size)
    down = left_down.reshape(2, eight, owners, pair, units)
    w3 = (down.transpose(0, 2, 1, 3, 4)[:, :, :, :, None, :] * eye[None, None, :, None, :, None]).reshape(2, size, size)
    w3t = (down.transpose(0, 1, 4, 2, 3)[:, :, :, :, None, :] * eye[None, :, None, None, :, None]).reshape(2, size, size)

    rows = pair * own_blocks
    flow = pltpu.VMEM((chunks, owners, rows, CHUNK), bf)
    vmem = pl.BlockSpec(memory_space=pltpu.VMEM)
    output, grad_tokens, sums = pl.pallas_call(
        functools.partial(kernel, chunks, owners),
        out_shape=(
            jax.ShapeDtypeStruct((deep, count), bf),
            jax.ShapeDtypeStruct((deep, count), bf),
            jax.ShapeDtypeStruct((3, wide, 128), jnp.float32),
        ),
        in_specs=[vmem] * 10,
        out_specs=(vmem, vmem, vmem),
        scratch_shapes=[
            flow, flow, flow, flow, flow, flow,
            pltpu.VMEM((2, size, CHUNK), bf),
            pltpu.VMEM((2, size, CHUNK), jnp.float32),
            pltpu.VMEM((2, size, CHUNK), bf),
            pltpu.VMEM((wide, 128), jnp.float32),
            pltpu.VMEM((wide, 128), jnp.float32),
            pltpu.VMEM((2, size, 128), jnp.float32),
            pltpu.VMEM((2, size, 128), jnp.float32),
            pltpu.VMEM((3, wide, 128), jnp.float32),
            pltpu.VMEM((3, wide // 2, 128), jnp.float32),
            pltpu.VMEM((3, wide // 2, 128), jnp.float32),
            pltpu.VMEM((3, wide // 2, 128), jnp.float32),
            pltpu.SemaphoreType.DMA((4, chunks)),
            pltpu.SemaphoreType.DMA((4, chunks)),
            pltpu.SemaphoreType.DMA((3, 3)),
            pltpu.SemaphoreType.DMA((3, 3)),
        ],
        compiler_params=pltpu.CompilerParams(
            collective_id=0, has_side_effects=True, vmem_limit_bytes=60 << 20
        ),
        name="monarch",
    )(
        tokens.reshape(deep, count), cotangent.reshape(deep, count),
        w1, w1t, w2, w2t, w3, w3t, w4, w4t,
    )
    sums = sums * factor
    both = sums[0].reshape(own_blocks, units, 128)
    grad_ld = both[:, :, :units]
    grad_lu = both[:, :, units:].transpose(0, 2, 1)
    grad_rd = sums[1].reshape(pair, hidden_blocks, width).transpose(0, 2, 1)
    grad_ru = sums[2].reshape(pair, hidden_blocks, width)
    shape = tokens.shape
    return (output.reshape(shape), grad_tokens.reshape(shape), grad_ru, grad_lu, grad_ld, grad_rd)


def solution(mesh):
    split = P("blk", None, "tok")
    whole = P("blk", None, None)
    return jax.shard_map(
        shards,
        mesh=mesh,
        in_specs=(split, split, whole, whole, whole, whole),
        out_specs=(split, split, whole, whole, whole, whole),
        check_vma=False,
    )
```

```python
import functools

import jax
import jax.numpy as jnp
from jax import lax
from jax.experimental import pallas as pl
from jax.experimental.pallas import tpu as pltpu
from jax.sharding import PartitionSpec as P

MESH = pl.DeviceIdType.MESH
CHUNK = 512
SPAN = 256
ROOT = 0.7978845608028654
CUBIC = 0.044715


def dot(a, b):
    return jnp.dot(a, b, preferred_element_type=jnp.float32)


def dot_nt(a, b):
    return lax.dot_general(a, b, (((1,), (1,)), ((), ())), preferred_element_type=jnp.float32)


def hops():
    near = lambda v: min(v, 4 - v)
    steps = [(x, z, y) for x in range(4) for z in range(4) for y in range(2)][1:]
    order = []
    for step in sorted(steps, key=lambda s: -(near(s[0]) + near(s[1]) + s[2])):
        for x, z in ((step[0], step[1]), (step[1], step[0])):
            for twin in ((x, z, step[2]), (-x % 4, -z % 4, step[2])):
                if twin not in order:
                    order.append(twin)
    return order


def neighbour(me, step):
    x, z, y = me // 8, lax.rem(me // 2, 4), lax.rem(me, 2)
    return (lax.rem(x + step[0], 4) * 4 + lax.rem(z + step[1], 4)) * 2 + lax.rem(y + step[2], 2)


def one_hot(test):
    return jnp.where(test, 1.0, 0.0).astype(jnp.bfloat16)


def square(size):
    row = lax.broadcasted_iota(jnp.int32, (size, size), 0)
    return one_hot(row == lax.broadcasted_iota(jnp.int32, (size, size), 1))


def kernel(
    chunks, owners, x_ref, cot_ref, ru_ref, lu_ref, ld_ref, rd_ref,
    out_ref, gt_ref, sums_ref,
    w1_ref, w1t_ref, w2_ref, w2t_ref, w3_ref, w3t_ref, w4_ref, w4t_ref,
    send_a, send_b, got_first, got_back, got_mixed, got_last, hidden, slope, back_pre,
    acc_ru, acc_rd, acc_ld, acc_lu, grads, near, own, far,
    send_sem, recv_sem, sum_send, sum_recv,
):
    me = lax.axis_index("blk")
    tok = lax.axis_index("tok")
    core_peer = tok + 1 - 2 * lax.rem(tok, 2)
    far_peer = tok + 2 - 4 * (tok // 2)
    rows = send_a.shape[2]
    half = rows // 2
    count = owners - 1
    others = [neighbour(me, step) for step in hops()]

    barrier = pltpu.get_barrier_semaphore()

    for to in others:
        pl.semaphore_signal(barrier, inc=1, device_id=(tok, to), device_id_type=MESH)
    pl.semaphore_signal(barrier, inc=1, device_id=(core_peer, me), device_id_type=MESH)
    pl.semaphore_signal(barrier, inc=1, device_id=(far_peer, me), device_id_type=MESH)

    for acc in (acc_ru, acc_rd, acc_ld, acc_lu):
        acc[...] = jnp.zeros_like(acc)

    def interleave():
        row = lax.broadcasted_iota(jnp.int32, (SPAN, SPAN // 2), 0)
        spot = 2 * lax.broadcasted_iota(jnp.int32, (SPAN, SPAN // 2), 1)
        for s in range(2):
            pick = one_hot(row == spot + s)
            for r in range(w1_ref.shape[0] // SPAN):
                at, part = slice(r * SPAN, (r + 1) * SPAN), slice(r * SPAN // 2, (r + 1) * SPAN // 2)
                lanes = slice(s * 128, (s + 1) * 128)
                w1_ref[at, lanes] = dot(pick, ru_ref[s, part, :]).astype(jnp.bfloat16)
                w4t_ref[at, lanes] = dot_nt(pick, rd_ref[s, :, part]).astype(jnp.bfloat16)

    def turned():
        flip = square(SPAN)
        for r in range(w1_ref.shape[0] // SPAN):
            at = slice(r * SPAN, (r + 1) * SPAN)
            w1t_ref[:, at] = dot_nt(flip, w1_ref[at, :]).astype(jnp.bfloat16)
            w4_ref[:, at] = dot_nt(flip, w4t_ref[at, :]).astype(jnp.bfloat16)

    def expand():
        units = lu_ref.shape[1]
        size = owners * half
        row = lax.broadcasted_iota(jnp.int32, (units, size), 0)
        col = lax.broadcasted_iota(jnp.int32, (units, size), 1)
        same = row == 2 * (col // half) + lax.rem(col, 2)
        block = lax.rem(col, half) // 2
        small = square(units)
        flip = square(SPAN)
        for c in range(half // 2):
            place = one_hot(same & (block == c))
            at = slice(c * units, (c + 1) * units)
            for h in range(2):
                index = h * (half // 2) + c
                w2_ref[h, at, :] = dot(lu_ref[index], place).astype(jnp.bfloat16)
                down = dot_nt(small, ld_ref[index]).astype(jnp.bfloat16)
                w3t_ref[h, at, :] = dot(down, place).astype(jnp.bfloat16)
        for h in range(2):
            for r in range(size // SPAN):
                for q in range(size // SPAN):
                    at, to = slice(r * SPAN, (r + 1) * SPAN), slice(q * SPAN, (q + 1) * SPAN)
                    w2t_ref[h, to, at] = dot_nt(flip, w2_ref[h, at, to]).astype(jnp.bfloat16)
                    w3_ref[h, to, at] = dot_nt(flip, w3t_ref[h, at, to]).astype(jnp.bfloat16)

    def columns(k):
        return pl.ds(pl.multiple_of(k * CHUNK, CHUNK), CHUNK)

    def post(kind, k, source, target):
        pltpu.make_async_copy(source.at[k, me], target.at[k, me], recv_sem.at[kind, k]).start()

        for to in others:
            pltpu.make_async_remote_copy(
                src_ref=source.at[k, to], dst_ref=target.at[k, me],
                send_sem=send_sem.at[kind, k], recv_sem=recv_sem.at[kind, k],
                device_id=(tok, to), device_id_type=MESH,
            ).start()

    def sent(kind, k, source):
        part = source.at[k, pl.ds(0, count)]
        pltpu.make_async_copy(part, part, send_sem.at[kind, k]).wait()

    def arrived(kind, k, target):
        pltpu.make_async_copy(target.at[k], target.at[k], recv_sem.at[kind, k]).wait()

    wide = SPAN // rows

    def spread(w_ref, data, buffer, k):
        def part(r, carry):
            w = w_ref[pl.ds(pl.multiple_of(r * SPAN, SPAN), SPAN), :]
            value = dot(w, data).astype(jnp.bfloat16)
            buffer[k, pl.ds(r * wide, wide)] = value.reshape(wide, rows, CHUNK)
            return carry

        lax.fori_loop(0, w_ref.shape[0] // SPAN, part, 0)

    def stage_first(k):
        spread(w1_ref, x_ref[:, columns(k)], send_a, k)

    def stage_back(k):
        spread(w4t_ref, cot_ref[:, columns(k)], send_b, k)

    def rows_of(buffer, k, h):
        return buffer[k, :, h * half:(h + 1) * half, :].reshape(owners * half, CHUNK)

    def keep_block(acc, h, r, value):
        which = lax.rem(lax.broadcasted_iota(jnp.int32, (SPAN, 128), 0), half) // 4
        kept = value[:, 0:128]
        for p in range(1, half // 4):
            kept = jnp.where(which == p, value[:, p * 128:(p + 1) * 128], kept)
        acc[h, r * SPAN:(r + 1) * SPAN, :] += kept

    def stage_middle(k):
        arrived(0, k, got_first)
        sent(0, k, send_a)
        size = owners * half
        for h in range(2):
            given = rows_of(got_first, k, h)
            for r in range(size // SPAN):
                at = pl.ds(r * SPAN, SPAN)
                pre = dot(w2_ref[h, at, :], given)
                square = pre * pre
                t = jnp.tanh(ROOT * (pre + CUBIC * (square * pre)))
                cdf = 0.5 * (1.0 + t)
                hidden[h, at, :] = (pre * cdf).astype(jnp.bfloat16)
                slope[h, at, :] = cdf + (0.5 * ROOT) * pre * (1.0 - t * t) * (1.0 + (3.0 * CUBIC) * square)
        each = SPAN // half
        for h in range(2):
            for r in range(size // SPAN):
                value = dot(w3_ref[h, pl.ds(r * SPAN, SPAN), :], hidden[h]).astype(jnp.bfloat16)
                send_a[k, r * each:(r + 1) * each, h * half:(h + 1) * half, :] = value.reshape(each, half, CHUNK)
        post(2, k, send_a, got_mixed)

        arrived(1, k, got_back)
        sent(1, k, send_b)
        for h in range(2):
            given = rows_of(got_back, k, h)
            for r in range(size // SPAN):
                at = pl.ds(r * SPAN, SPAN)
                back = dot(w3t_ref[h, at, :], given)
                back_pre[h, at, :] = (back * slope[h, at, :]).astype(jnp.bfloat16)
        for h in range(2):
            for r in range(size // SPAN):
                value = dot(w2t_ref[h, pl.ds(r * SPAN, SPAN), :], back_pre[h]).astype(jnp.bfloat16)
                send_b[k, r * each:(r + 1) * each, h * half:(h + 1) * half, :] = value.reshape(each, half, CHUNK)
        post(3, k, send_b, got_last)

        for h in range(2):
            for r in range(size // SPAN):
                part = slice(r * each, (r + 1) * each)
                inner = slice(h * half, (h + 1) * half)
                back = got_back[k, part, inner, :].reshape(SPAN, CHUNK)
                keep_block(acc_ld, h, r, dot_nt(back, hidden[h]))
                first = got_first[k, part, inner, :].reshape(SPAN, CHUNK)
                keep_block(acc_lu, h, r, dot_nt(first, back_pre[h]))

    def gather(k, got, w_ref, data_ref, into_ref, acc):
        data = data_ref[:, columns(k)]
        everything = got[k].reshape(owners * rows, CHUNK)
        into_ref[:, columns(k)] = dot(w_ref[...], everything).astype(jnp.bfloat16)
        odd = lax.rem(lax.broadcasted_iota(jnp.int32, (SPAN, 128), 0), 2) == 1

        def part(r, carry):
            piece = got[k, pl.ds(r * wide, wide)].reshape(SPAN, CHUNK)
            value = dot_nt(piece, data)
            at = pl.ds(pl.multiple_of(r * SPAN, SPAN), SPAN)
            acc[at, :] += jnp.where(odd, value[:, 128:256], value[:, 0:128])
            return carry

        lax.fori_loop(0, owners * rows // SPAN, part, 0)

    def stage_output(k):
        arrived(2, k, got_mixed)
        gather(k, got_mixed, w4_ref, cot_ref, out_ref, acc_rd)

    def stage_grad(k):
        arrived(3, k, got_last)
        gather(k, got_last, w1t_ref, x_ref, gt_ref, acc_ru)

    interleave()
    stage_first(0)
    stage_back(0)
    pl.semaphore_wait(barrier, count + 2)
    post(0, 0, send_a, got_first)
    post(1, 0, send_b, got_back)

    def ahead(k):
        stage_first(k)
        post(0, k, send_a, got_first)
        stage_back(k)
        post(1, k, send_b, got_back)

    ahead(1)
    expand()
    turned()

    def step(k, carry):
        stage_middle(k)

        @pl.when(k + 2 < chunks)
        def _():
            ahead(k + 2)

        @pl.when(k >= 1)
        def _():
            stage_output(k - 1)
            stage_grad(k - 1)

        return carry

    lax.fori_loop(0, chunks, step, 0)

    part = grads.shape[1] // 2
    core = lax.rem(tok, 2)
    mine = pl.ds(pl.multiple_of(core * part, part), part)
    theirs = pl.ds(pl.multiple_of(part - core * part, part), part)

    def pair(i):
        return pltpu.make_async_remote_copy(
            src_ref=grads.at[i, theirs], dst_ref=near.at[i], send_sem=sum_send.at[0, i], recv_sem=sum_recv.at[0, i],
            device_id=(core_peer, me), device_id_type=MESH,
        )

    def across(i):
        return pltpu.make_async_remote_copy(
            src_ref=own.at[i], dst_ref=far.at[i], send_sem=sum_send.at[1, i], recv_sem=sum_recv.at[1, i],
            device_id=(far_peer, me), device_id_type=MESH,
        )

    def share(i):
        return pltpu.make_async_remote_copy(
            src_ref=sums_ref.at[i, mine], dst_ref=sums_ref.at[i, mine],
            send_sem=sum_send.at[2, i], recv_sem=sum_recv.at[2, i],
            device_id=(core_peer, me), device_id_type=MESH,
        )

    def begin(i):
        pair(i).start()

    def middle(i):
        pair(i).wait()
        own[i] = grads[i, mine, :] + near[i]
        across(i).start()

    def finish(i):
        across(i).wait()
        sums_ref[i, mine, :] = own[i] + far[i]
        share(i).start()

    lane = lax.broadcasted_iota(jnp.int32, (owners, 128), 1)
    for h in range(2):
        for c in range(half // 2):
            for s in range(2):
                ld = acc_ld[h, pl.ds(2 * c + s, owners, stride=half), :]
                lu = acc_lu[h, pl.ds(2 * c + s, owners, stride=half), :]
                if c % 2 == 0:
                    both = jnp.where(lane < 64, ld, pltpu.roll(lu, 64, 1))
                else:
                    both = jnp.where(lane < 64, pltpu.roll(ld, 64, 1), lu)
                base = (h * (half // 2) + c) * 2 * owners
                grads[0, pl.ds(base + s, owners, stride=2), :] = both
    begin(0)

    size = owners * half
    last = chunks - 1
    stage_output(last)
    for s in range(2):
        grads[1, s * size:(s + 1) * size, :] = acc_rd[pl.ds(s, size, stride=2), :]
    begin(1)
    middle(0)
    middle(1)
    stage_grad(last)
    for s in range(2):
        grads[2, s * size:(s + 1) * size, :] = acc_ru[pl.ds(s, size, stride=2), :]
    begin(2)
    finish(0)
    finish(1)
    middle(2)
    finish(2)

    def drain(k, carry):
        sent(2, k, send_a)
        sent(3, k, send_b)
        return carry

    lax.fori_loop(0, chunks, drain, 0)
    for i in range(3):
        share(i).wait()


def shards(tokens, cotangent, right_up, left_up, left_down, right_down):
    tok_count = lax.axis_size("tok")
    owners = lax.axis_size("blk")
    factor = float(tokens.shape[2] * tok_count) ** (-0.5)
    pair, width, count = tokens.shape
    hidden_blocks = right_up.shape[1]
    own_blocks = left_up.shape[0]
    units = left_up.shape[1]
    eight = own_blocks // 2
    chunks = count // CHUNK
    bf = jnp.bfloat16

    wide, deep = pair * hidden_blocks, pair * width
    size = eight * units
    rows = pair * own_blocks
    flow = pltpu.VMEM((chunks, owners, rows, CHUNK), bf)
    vmem = pl.BlockSpec(memory_space=pltpu.VMEM)
    output, grad_tokens, sums = pl.pallas_call(
        functools.partial(kernel, chunks, owners),
        out_shape=(
            jax.ShapeDtypeStruct((deep, count), bf),
            jax.ShapeDtypeStruct((deep, count), bf),
            jax.ShapeDtypeStruct((3, wide, 128), jnp.float32),
        ),
        in_specs=[vmem] * 6,
        out_specs=(vmem, vmem, vmem),
        scratch_shapes=[
            pltpu.VMEM((wide, deep), bf), pltpu.VMEM((deep, wide), bf),
            pltpu.VMEM((2, size, size), bf), pltpu.VMEM((2, size, size), bf),
            pltpu.VMEM((2, size, size), bf), pltpu.VMEM((2, size, size), bf),
            pltpu.VMEM((deep, wide), bf), pltpu.VMEM((wide, deep), bf),
            flow, flow, flow, flow, flow, flow,
            pltpu.VMEM((2, size, CHUNK), bf),
            pltpu.VMEM((2, size, CHUNK), jnp.float32),
            pltpu.VMEM((2, size, CHUNK), bf),
            pltpu.VMEM((wide, 128), jnp.float32),
            pltpu.VMEM((wide, 128), jnp.float32),
            pltpu.VMEM((2, size, 128), jnp.float32),
            pltpu.VMEM((2, size, 128), jnp.float32),
            pltpu.VMEM((3, wide, 128), jnp.float32),
            pltpu.VMEM((3, wide // 2, 128), jnp.float32),
            pltpu.VMEM((3, wide // 2, 128), jnp.float32),
            pltpu.VMEM((3, wide // 2, 128), jnp.float32),
            pltpu.SemaphoreType.DMA((4, chunks)),
            pltpu.SemaphoreType.DMA((4, chunks)),
            pltpu.SemaphoreType.DMA((3, 3)),
            pltpu.SemaphoreType.DMA((3, 3)),
        ],
        compiler_params=pltpu.CompilerParams(
            collective_id=0, has_side_effects=True, vmem_limit_bytes=60 << 20
        ),
        name="monarch",
    )(
        tokens.reshape(deep, count), cotangent.reshape(deep, count),
        right_up, left_up, left_down, right_down,
    )
    sums = sums * factor
    both = sums[0].reshape(own_blocks, units, 128)
    grad_ld = both[:, :, :units]
    grad_lu = both[:, :, units:].transpose(0, 2, 1)
    grad_rd = sums[1].reshape(pair, hidden_blocks, width).transpose(0, 2, 1)
    grad_ru = sums[2].reshape(pair, hidden_blocks, width)
    shape = tokens.shape
    return (output.reshape(shape), grad_tokens.reshape(shape), grad_ru, grad_lu, grad_ld, grad_rd)


def solution(mesh):
    split = P("blk", None, "tok")
    whole = P("blk", None, None)
    return jax.shard_map(
        shards,
        mesh=mesh,
        in_specs=(split, split, whole, whole, whole, whole),
        out_specs=(split, split, whole, whole, whole, whole),
        check_vma=False,
    )
```

```python
import functools

import jax
import jax.numpy as jnp
from jax import lax
from jax.experimental import pallas as pl
from jax.experimental.pallas import tpu as pltpu
from jax.sharding import PartitionSpec as P

MESH = pl.DeviceIdType.MESH
CHUNK = 256
AHEAD = 4
LAG = 2
SPAN = 256
ROOT = 0.7978845608028654
CUBIC = 0.044715


def dot(a, b):
    return jnp.dot(a, b, preferred_element_type=jnp.float32)


def dot_nt(a, b):
    return lax.dot_general(a, b, (((1,), (1,)), ((), ())), preferred_element_type=jnp.float32)


def hops():
    near = lambda v: min(v, 4 - v)
    steps = [(x, z, y) for x in range(4) for z in range(4) for y in range(2)][1:]
    order = []
    for step in sorted(steps, key=lambda s: -(near(s[0]) + near(s[1]) + s[2])):
        for x, z in ((step[0], step[1]), (step[1], step[0])):
            for twin in ((x, z, step[2]), (-x % 4, -z % 4, step[2])):
                if twin not in order:
                    order.append(twin)
    return order


def neighbour(me, step):
    x, z, y = me // 8, lax.rem(me // 2, 4), lax.rem(me, 2)
    return (lax.rem(x + step[0], 4) * 4 + lax.rem(z + step[1], 4)) * 2 + lax.rem(y + step[2], 2)


def one_hot(test):
    return jnp.where(test, 1.0, 0.0).astype(jnp.bfloat16)


def square(size):
    row = lax.broadcasted_iota(jnp.int32, (size, size), 0)
    return one_hot(row == lax.broadcasted_iota(jnp.int32, (size, size), 1))


def kernel(
    chunks, owners, x_hbm, cot_hbm, ru_ref, rd_ref, lu_hbm, ld_hbm,
    out_hbm, gt_hbm, sums_ref,
    x_ref, cot_ref, lu_ref, ld_ref, out_ref, gt_ref,
    w1_ref, w1t_ref, w2_ref, w2t_ref, w3_ref, w3t_ref, w4_ref, w4t_ref,
    send_a, send_b, got_first, got_back, got_mixed, got_last, hidden, slope, back_pre,
    acc_ru, acc_rd, acc_ld, acc_lu, grads, near, own, far,
    send_sem, recv_sem, sum_send, sum_recv, in_sem, out_sem,
):
    me = lax.axis_index("blk")
    tok = lax.axis_index("tok")
    core_peer = tok + 1 - 2 * lax.rem(tok, 2)
    far_peer = tok + 2 - 4 * (tok // 2)
    rows = send_a.shape[2]
    half = rows // 2
    count = owners - 1
    others = [neighbour(me, step) for step in hops()]

    def columns(k):
        return pl.ds(pl.multiple_of(k * CHUNK, CHUNK), CHUNK)

    head, tail = pl.ds(0, CHUNK), pl.ds(CHUNK, x_ref.shape[1] - CHUNK)
    loads = [
        pltpu.make_async_copy(x_hbm.at[:, head], x_ref.at[:, head], in_sem.at[0]),
        pltpu.make_async_copy(cot_hbm.at[:, head], cot_ref.at[:, head], in_sem.at[1]),
        pltpu.make_async_copy(x_hbm.at[:, tail], x_ref.at[:, tail], in_sem.at[2]),
        pltpu.make_async_copy(cot_hbm.at[:, tail], cot_ref.at[:, tail], in_sem.at[3]),
        pltpu.make_async_copy(lu_hbm, lu_ref, in_sem.at[4]),
        pltpu.make_async_copy(ld_hbm, ld_ref, in_sem.at[5]),
    ]
    for load in loads:
        load.start()

    barrier = pltpu.get_barrier_semaphore()

    for to in others:
        pl.semaphore_signal(barrier, inc=1, device_id=(tok, to), device_id_type=MESH)
    pl.semaphore_signal(barrier, inc=1, device_id=(core_peer, me), device_id_type=MESH)
    pl.semaphore_signal(barrier, inc=1, device_id=(far_peer, me), device_id_type=MESH)

    def interleave():
        row = lax.broadcasted_iota(jnp.int32, (SPAN, SPAN // 2), 0)
        spot = 2 * lax.broadcasted_iota(jnp.int32, (SPAN, SPAN // 2), 1)
        for s in range(2):
            pick = one_hot(row == spot + s)
            for r in range(w1_ref.shape[0] // SPAN):
                at, part = slice(r * SPAN, (r + 1) * SPAN), slice(r * SPAN // 2, (r + 1) * SPAN // 2)
                lanes = slice(s * 128, (s + 1) * 128)
                w1_ref[at, lanes] = dot(pick, ru_ref[s, part, :]).astype(jnp.bfloat16)
                w4t_ref[at, lanes] = dot_nt(pick, rd_ref[s, :, part]).astype(jnp.bfloat16)

    def turned():
        flip = square(SPAN)
        for r in range(w1_ref.shape[0] // SPAN):
            at = slice(r * SPAN, (r + 1) * SPAN)
            w1t_ref[:, at] = dot_nt(flip, w1_ref[at, :]).astype(jnp.bfloat16)
            w4_ref[:, at] = dot_nt(flip, w4t_ref[at, :]).astype(jnp.bfloat16)

    def expand():
        units = lu_ref.shape[1]
        size = owners * half
        row = lax.broadcasted_iota(jnp.int32, (units, size), 0)
        col = lax.broadcasted_iota(jnp.int32, (units, size), 1)
        same = row == 2 * (col // half) + lax.rem(col, 2)
        block = lax.rem(col, half) // 2
        small = square(units)
        flip = square(SPAN)
        for c in range(half // 2):
            place = one_hot(same & (block == c))
            at = slice(c * units, (c + 1) * units)
            for h in range(2):
                index = h * (half // 2) + c
                w2_ref[h, at, :] = dot(lu_ref[index], place).astype(jnp.bfloat16)
                down = dot_nt(small, ld_ref[index]).astype(jnp.bfloat16)
                w3t_ref[h, at, :] = dot(down, place).astype(jnp.bfloat16)
        for h in range(2):
            for r in range(size // SPAN):
                for q in range(size // SPAN):
                    at, to = slice(r * SPAN, (r + 1) * SPAN), slice(q * SPAN, (q + 1) * SPAN)
                    w2t_ref[h, to, at] = dot_nt(flip, w2_ref[h, at, to]).astype(jnp.bfloat16)
                    w3_ref[h, to, at] = dot_nt(flip, w3t_ref[h, at, to]).astype(jnp.bfloat16)

    def post(kind, k, source, target):
        pltpu.make_async_copy(source.at[k, me], target.at[k, me], recv_sem.at[kind, k]).start()

        for to in others:
            pltpu.make_async_remote_copy(
                src_ref=source.at[k, to], dst_ref=target.at[k, me],
                send_sem=send_sem.at[kind, k], recv_sem=recv_sem.at[kind, k],
                device_id=(tok, to), device_id_type=MESH,
            ).start()

    def sent(kind, k, source):
        part = source.at[k, pl.ds(0, count)]
        pltpu.make_async_copy(part, part, send_sem.at[kind, k]).wait()

    def arrived(kind, k, target):
        pltpu.make_async_copy(target.at[k], target.at[k], recv_sem.at[kind, k]).wait()

    wide = SPAN // rows

    def spread(w_ref, data, buffer, k):
        def part(r, carry):
            w = w_ref[pl.ds(pl.multiple_of(r * SPAN, SPAN), SPAN), :]
            value = dot(w, data).astype(jnp.bfloat16)
            buffer[k, pl.ds(r * wide, wide)] = value.reshape(wide, rows, CHUNK)
            return carry

        lax.fori_loop(0, w_ref.shape[0] // SPAN, part, 0)

    def stage_first(k):
        spread(w1_ref, x_ref[:, columns(k)], send_a, k)

    def stage_back(k):
        spread(w4t_ref, cot_ref[:, columns(k)], send_b, k)

    def rows_of(buffer, k, h):
        return buffer[k, :, h * half:(h + 1) * half, :].reshape(owners * half, CHUNK)

    def keep_block(acc, h, r, value):
        which = lax.rem(lax.broadcasted_iota(jnp.int32, (SPAN, 128), 0), half) // 4
        kept = value[:, 0:128]
        for p in range(1, half // 4):
            kept = jnp.where(which == p, value[:, p * 128:(p + 1) * 128], kept)
        acc[h, r * SPAN:(r + 1) * SPAN, :] += kept

    def stage_middle(k):
        arrived(0, k, got_first)
        sent(0, k, send_a)
        size = owners * half
        for h in range(2):
            given = rows_of(got_first, k, h)
            for r in range(size // SPAN):
                at = pl.ds(r * SPAN, SPAN)
                pre = dot(w2_ref[h, at, :], given)
                square = pre * pre
                t = jnp.tanh(ROOT * (pre + CUBIC * (square * pre)))
                cdf = 0.5 * (1.0 + t)
                hidden[h, at, :] = (pre * cdf).astype(jnp.bfloat16)
                slope[h, at, :] = cdf + (0.5 * ROOT) * pre * (1.0 - t * t) * (1.0 + (3.0 * CUBIC) * square)
        each = SPAN // half
        for h in range(2):
            for r in range(size // SPAN):
                value = dot(w3_ref[h, pl.ds(r * SPAN, SPAN), :], hidden[h]).astype(jnp.bfloat16)
                send_a[k, r * each:(r + 1) * each, h * half:(h + 1) * half, :] = value.reshape(each, half, CHUNK)
        post(2, k, send_a, got_mixed)

        arrived(1, k, got_back)
        sent(1, k, send_b)
        for h in range(2):
            given = rows_of(got_back, k, h)
            for r in range(size // SPAN):
                at = pl.ds(r * SPAN, SPAN)
                back = dot(w3t_ref[h, at, :], given)
                back_pre[h, at, :] = (back * slope[h, at, :]).astype(jnp.bfloat16)
        for h in range(2):
            for r in range(size // SPAN):
                value = dot(w2t_ref[h, pl.ds(r * SPAN, SPAN), :], back_pre[h]).astype(jnp.bfloat16)
                send_b[k, r * each:(r + 1) * each, h * half:(h + 1) * half, :] = value.reshape(each, half, CHUNK)
        post(3, k, send_b, got_last)

        for h in range(2):
            for r in range(size // SPAN):
                part = slice(r * each, (r + 1) * each)
                inner = slice(h * half, (h + 1) * half)
                back = got_back[k, part, inner, :].reshape(SPAN, CHUNK)
                keep_block(acc_ld, h, r, dot_nt(back, hidden[h]))
                first = got_first[k, part, inner, :].reshape(SPAN, CHUNK)
                keep_block(acc_lu, h, r, dot_nt(first, back_pre[h]))

    def apply(k, got, w_ref, into_ref):
        everything = got[k].reshape(owners * rows, CHUNK)
        into_ref[:, columns(k)] = dot(w_ref[...], everything).astype(jnp.bfloat16)

    def collect(k, got, data_ref, acc):
        data = data_ref[:, columns(k)]
        odd = lax.rem(lax.broadcasted_iota(jnp.int32, (SPAN, 128), 0), 2) == 1

        def part(r, carry):
            piece = got[k, pl.ds(r * wide, wide)].reshape(SPAN, CHUNK)
            value = dot_nt(piece, data)
            at = pl.ds(pl.multiple_of(r * SPAN, SPAN), SPAN)
            acc[at, :] += jnp.where(odd, value[:, 128:256], value[:, 0:128])
            return carry

        lax.fori_loop(0, owners * rows // SPAN, part, 0)

    def save_out(k):
        return pltpu.make_async_copy(out_ref.at[:, columns(k)], out_hbm.at[:, columns(k)], out_sem.at[0, k])

    def save_gt(k):
        return pltpu.make_async_copy(gt_ref.at[:, columns(k)], gt_hbm.at[:, columns(k)], out_sem.at[1, k])

    def stage_output(k):
        apply(k, got_mixed, w4_ref, out_ref)
        save_out(k).start()

    def stage_grad(k):
        apply(k, got_last, w1t_ref, gt_ref)
        save_gt(k).start()

    def sum_output(k):
        arrived(2, k, got_mixed)
        collect(k, got_mixed, cot_ref, acc_rd)

    def sum_grad(k):
        arrived(3, k, got_last)
        collect(k, got_last, x_ref, acc_ru)

    interleave()
    loads[0].wait()
    stage_first(0)
    loads[1].wait()
    stage_back(0)
    pl.semaphore_wait(barrier, count + 2)
    post(0, 0, send_a, got_first)
    post(1, 0, send_b, got_back)
    loads[2].wait()
    loads[3].wait()

    def ahead(k):
        stage_first(k)
        post(0, k, send_a, got_first)
        stage_back(k)
        post(1, k, send_b, got_back)

    for k in range(1, AHEAD):
        ahead(k)
    for acc in (acc_ru, acc_rd, acc_ld, acc_lu):
        acc[...] = jnp.zeros_like(acc)
    loads[4].wait()
    loads[5].wait()
    expand()
    turned()

    def step(k, carry):
        stage_middle(k)

        @pl.when(k + AHEAD < chunks)
        def _():
            ahead(k + AHEAD)

        @pl.when(k >= LAG)
        def _():
            sum_output(k - LAG)
            stage_output(k - LAG)
            sum_grad(k - LAG)
            stage_grad(k - LAG)

        return carry

    lax.fori_loop(0, chunks, step, 0)

    part = grads.shape[1] // 2
    core = lax.rem(tok, 2)
    mine = pl.ds(pl.multiple_of(core * part, part), part)
    theirs = pl.ds(pl.multiple_of(part - core * part, part), part)

    def pair(i):
        return pltpu.make_async_remote_copy(
            src_ref=grads.at[i, theirs], dst_ref=near.at[i], send_sem=sum_send.at[0, i], recv_sem=sum_recv.at[0, i],
            device_id=(core_peer, me), device_id_type=MESH,
        )

    def across(i):
        return pltpu.make_async_remote_copy(
            src_ref=own.at[i], dst_ref=far.at[i], send_sem=sum_send.at[1, i], recv_sem=sum_recv.at[1, i],
            device_id=(far_peer, me), device_id_type=MESH,
        )

    def share(i):
        return pltpu.make_async_remote_copy(
            src_ref=sums_ref.at[i, mine], dst_ref=sums_ref.at[i, mine],
            send_sem=sum_send.at[2, i], recv_sem=sum_recv.at[2, i],
            device_id=(core_peer, me), device_id_type=MESH,
        )

    def begin(i):
        pair(i).start()

    def middle(i):
        pair(i).wait()
        own[i] = (grads[i, mine, :] + near[i]).astype(jnp.bfloat16)
        across(i).start()

    def finish(i):
        across(i).wait()
        sums_ref[i, mine, :] = own[i].astype(jnp.float32) + far[i].astype(jnp.float32)
        share(i).start()

    lane = lax.broadcasted_iota(jnp.int32, (owners, 128), 1)
    for h in range(2):
        for c in range(half // 2):
            for s in range(2):
                ld = acc_ld[h, pl.ds(2 * c + s, owners, stride=half), :]
                lu = acc_lu[h, pl.ds(2 * c + s, owners, stride=half), :]
                if c % 2 == 0:
                    both = jnp.where(lane < 64, ld, pltpu.roll(lu, 64, 1))
                else:
                    both = jnp.where(lane < 64, pltpu.roll(ld, 64, 1), lu)
                base = (h * (half // 2) + c) * 2 * owners
                grads[0, pl.ds(base + s, owners, stride=2), :] = both
    begin(0)

    size = owners * half
    last = chunks - 1
    for k in range(chunks - LAG, last):
        sum_output(k)
        stage_output(k)
        sum_grad(k)
        stage_grad(k)
    sum_output(last)
    for s in range(2):
        grads[1, s * size:(s + 1) * size, :] = acc_rd[pl.ds(s, size, stride=2), :]
    begin(1)
    middle(0)
    stage_output(last)
    middle(1)
    sum_grad(last)
    for s in range(2):
        grads[2, s * size:(s + 1) * size, :] = acc_ru[pl.ds(s, size, stride=2), :]
    begin(2)
    stage_grad(last)
    middle(2)
    finish(0)
    finish(1)
    finish(2)

    def drain(k, carry):
        sent(2, k, send_a)
        sent(3, k, send_b)
        save_out(k).wait()
        save_gt(k).wait()
        return carry

    lax.fori_loop(0, chunks, drain, 0)
    for i in range(3):
        share(i).wait()


def finish(factor, out_hbm, gt_hbm, sums_ref, out_to, gt_to, ru_ref, lu_ref, ld_ref, rd_ref, sem):
    copies = [pltpu.make_async_copy(out_hbm, out_to, sem.at[0]), pltpu.make_async_copy(gt_hbm, gt_to, sem.at[1])]
    for copy in copies:
        copy.start()
    units = ld_ref.shape[1]
    size = sums_ref.shape[1] // 2
    for c in range(ld_ref.shape[0]):
        both = sums_ref[0, c * units:(c + 1) * units, :] * factor
        ld_ref[c] = both[:, :units]
        lu_ref[c] = both.T[units:, :]
    for s in range(2):
        part = slice(s * size, (s + 1) * size)
        rd_ref[s] = (sums_ref[1, part, :] * factor).T
        ru_ref[s] = sums_ref[2, part, :] * factor
    for copy in copies:
        copy.wait()


def shards(tokens, cotangent, right_up, left_up, left_down, right_down):
    tok_count = lax.axis_size("tok")
    owners = lax.axis_size("blk")
    factor = float(tokens.shape[2] * tok_count) ** (-0.5)
    pair, width, count = tokens.shape
    hidden_blocks = right_up.shape[1]
    own_blocks = left_up.shape[0]
    units = left_up.shape[1]
    eight = own_blocks // 2
    chunks = count // CHUNK
    bf = jnp.bfloat16

    wide, deep = pair * hidden_blocks, pair * width
    size = eight * units
    rows = pair * own_blocks
    flow = pltpu.VMEM((chunks, owners, rows, CHUNK), bf)
    vmem = pl.BlockSpec(memory_space=pltpu.VMEM)
    hbm = pl.BlockSpec(memory_space=pltpu.HBM)
    output, grad_tokens, sums = pl.pallas_call(
        functools.partial(kernel, chunks, owners),
        out_shape=(
            jax.ShapeDtypeStruct((deep, count), bf),
            jax.ShapeDtypeStruct((deep, count), bf),
            jax.ShapeDtypeStruct((3, wide, 128), jnp.float32),
        ),
        in_specs=[hbm, hbm, vmem, vmem, hbm, hbm],
        out_specs=(hbm, hbm, vmem),
        scratch_shapes=[
            pltpu.VMEM((deep, count), bf), pltpu.VMEM((deep, count), bf),
            pltpu.VMEM(left_up.shape, bf), pltpu.VMEM(left_down.shape, bf),
            pltpu.VMEM((deep, count), bf), pltpu.VMEM((deep, count), bf),
            pltpu.VMEM((wide, deep), bf), pltpu.VMEM((deep, wide), bf),
            pltpu.VMEM((2, size, size), bf), pltpu.VMEM((2, size, size), bf),
            pltpu.VMEM((2, size, size), bf), pltpu.VMEM((2, size, size), bf),
            pltpu.VMEM((deep, wide), bf), pltpu.VMEM((wide, deep), bf),
            flow, flow, flow, flow, flow, flow,
            pltpu.VMEM((2, size, CHUNK), bf),
            pltpu.VMEM((2, size, CHUNK), jnp.float32),
            pltpu.VMEM((2, size, CHUNK), bf),
            pltpu.VMEM((wide, 128), jnp.float32),
            pltpu.VMEM((wide, 128), jnp.float32),
            pltpu.VMEM((2, size, 128), jnp.float32),
            pltpu.VMEM((2, size, 128), jnp.float32),
            pltpu.VMEM((3, wide, 128), jnp.float32),
            pltpu.VMEM((3, wide // 2, 128), jnp.float32),
            pltpu.VMEM((3, wide // 2, 128), bf),
            pltpu.VMEM((3, wide // 2, 128), bf),
            pltpu.SemaphoreType.DMA((4, chunks)),
            pltpu.SemaphoreType.DMA((4, chunks)),
            pltpu.SemaphoreType.DMA((3, 3)),
            pltpu.SemaphoreType.DMA((3, 3)),
            pltpu.SemaphoreType.DMA((6,)),
            pltpu.SemaphoreType.DMA((2, chunks)),
        ],
        compiler_params=pltpu.CompilerParams(
            collective_id=0, has_side_effects=True, vmem_limit_bytes=60 << 20
        ),
        name="monarch",
    )(
        tokens.reshape(deep, count), cotangent.reshape(deep, count),
        right_up, right_down, left_up, left_down,
    )
    shape = tokens.shape
    output, grad_tokens, grad_ru, grad_lu, grad_ld, grad_rd = pl.pallas_call(
        functools.partial(finish, factor),
        out_shape=(
            jax.ShapeDtypeStruct((deep, count), bf),
            jax.ShapeDtypeStruct((deep, count), bf),
            jax.ShapeDtypeStruct(right_up.shape, jnp.float32),
            jax.ShapeDtypeStruct(left_up.shape, jnp.float32),
            jax.ShapeDtypeStruct(left_down.shape, jnp.float32),
            jax.ShapeDtypeStruct(right_down.shape, jnp.float32),
        ),
        in_specs=[hbm, hbm, vmem],
        out_specs=(hbm, hbm, vmem, vmem, vmem, vmem),
        scratch_shapes=[pltpu.SemaphoreType.DMA((2,))],
        compiler_params=pltpu.CompilerParams(vmem_limit_bytes=16 << 20),
        name="finish",
    )(output, grad_tokens, sums)
    return (output.reshape(shape), grad_tokens.reshape(shape), grad_ru, grad_lu, grad_ld, grad_rd)


def solution(mesh):
    split = P("blk", None, "tok")
    whole = P("blk", None, None)
    return jax.shard_map(
        shards,
        mesh=mesh,
        in_specs=(split, split, whole, whole, whole, whole),
        out_specs=(split, split, whole, whole, whole, whole),
        check_vma=False,
    )
```

```python
import functools

import jax
import jax.numpy as jnp
from jax import lax
from jax.experimental import pallas as pl
from jax.experimental.pallas import tpu as pltpu
from jax.sharding import PartitionSpec as P

MESH = pl.DeviceIdType.MESH
CHUNK = 256
AHEAD = 4
LAG = 2
SPAN = 256
ROOT = 0.7978845608028654
CUBIC = 0.044715


def dot(a, b):
    return jnp.dot(a, b, preferred_element_type=jnp.float32)


def dot_nt(a, b):
    return lax.dot_general(a, b, (((1,), (1,)), ((), ())), preferred_element_type=jnp.float32)


def hops():
    near = lambda v: min(v, 4 - v)
    steps = [(x, z, y) for x in range(4) for z in range(4) for y in range(2)][1:]
    order = []
    for step in sorted(steps, key=lambda s: -(near(s[0]) + near(s[1]) + s[2])):
        for x, z in ((step[0], step[1]), (step[1], step[0])):
            for twin in ((x, z, step[2]), (-x % 4, -z % 4, step[2])):
                if twin not in order:
                    order.append(twin)
    return order


def neighbour(me, step):
    x, z, y = me // 8, lax.rem(me // 2, 4), lax.rem(me, 2)
    return (lax.rem(x + step[0], 4) * 4 + lax.rem(z + step[1], 4)) * 2 + lax.rem(y + step[2], 2)


def one_hot(test):
    return jnp.where(test, 1.0, 0.0).astype(jnp.bfloat16)


def square(size):
    row = lax.broadcasted_iota(jnp.int32, (size, size), 0)
    return one_hot(row == lax.broadcasted_iota(jnp.int32, (size, size), 1))


def kernel(
    chunks, owners, x_hbm, cot_hbm, ru_ref, rd_ref, lu_hbm, ld_hbm,
    out_hbm, gt_hbm, sums_hbm,
    x_ref, cot_ref, lu_ref, ld_ref, out_ref, gt_ref,
    w1_ref, w1t_ref, w2_ref, w2t_ref, w3_ref, w3t_ref, w4_ref, w4t_ref,
    send_a, send_b, got_first, got_back, got_mixed, got_last, hidden, slope, back_pre,
    acc_ru, acc_rd, acc_ld, acc_lu, grads, near, own, far, sums_ref,
    send_sem, recv_sem, sum_send, sum_recv, in_sem, out_sem, save_sem,
):
    me = lax.axis_index("blk")
    tok = lax.axis_index("tok")
    core_peer = tok + 1 - 2 * lax.rem(tok, 2)
    far_peer = tok + 2 - 4 * (tok // 2)
    rows = send_a.shape[2]
    half = rows // 2
    count = owners - 1
    others = [neighbour(me, step) for step in hops()]

    def columns(k):
        return pl.ds(pl.multiple_of(k * CHUNK, CHUNK), CHUNK)

    head, tail = pl.ds(0, CHUNK), pl.ds(CHUNK, x_ref.shape[1] - CHUNK)
    loads = [
        pltpu.make_async_copy(x_hbm.at[:, head], x_ref.at[:, head], in_sem.at[0]),
        pltpu.make_async_copy(cot_hbm.at[:, head], cot_ref.at[:, head], in_sem.at[1]),
        pltpu.make_async_copy(x_hbm.at[:, tail], x_ref.at[:, tail], in_sem.at[2]),
        pltpu.make_async_copy(cot_hbm.at[:, tail], cot_ref.at[:, tail], in_sem.at[3]),
        pltpu.make_async_copy(lu_hbm, lu_ref, in_sem.at[4]),
        pltpu.make_async_copy(ld_hbm, ld_ref, in_sem.at[5]),
    ]
    for load in loads:
        load.start()

    barrier = pltpu.get_barrier_semaphore()

    for to in others:
        pl.semaphore_signal(barrier, inc=1, device_id=(tok, to), device_id_type=MESH)
    pl.semaphore_signal(barrier, inc=1, device_id=(core_peer, me), device_id_type=MESH)
    pl.semaphore_signal(barrier, inc=1, device_id=(far_peer, me), device_id_type=MESH)

    def interleave():
        row = lax.broadcasted_iota(jnp.int32, (SPAN, SPAN // 2), 0)
        spot = 2 * lax.broadcasted_iota(jnp.int32, (SPAN, SPAN // 2), 1)
        for s in range(2):
            pick = one_hot(row == spot + s)
            for r in range(w1_ref.shape[0] // SPAN):
                at, part = slice(r * SPAN, (r + 1) * SPAN), slice(r * SPAN // 2, (r + 1) * SPAN // 2)
                lanes = slice(s * 128, (s + 1) * 128)
                w1_ref[at, lanes] = dot(pick, ru_ref[s, part, :]).astype(jnp.bfloat16)
                w4t_ref[at, lanes] = dot_nt(pick, rd_ref[s, :, part]).astype(jnp.bfloat16)

    def turned():
        flip = square(SPAN)
        for r in range(w1_ref.shape[0] // SPAN):
            at = slice(r * SPAN, (r + 1) * SPAN)
            w1t_ref[:, at] = dot_nt(flip, w1_ref[at, :]).astype(jnp.bfloat16)
            w4_ref[:, at] = dot_nt(flip, w4t_ref[at, :]).astype(jnp.bfloat16)

    def expand():
        units = lu_ref.shape[1]
        size = owners * half
        row = lax.broadcasted_iota(jnp.int32, (units, size), 0)
        col = lax.broadcasted_iota(jnp.int32, (units, size), 1)
        same = row == 2 * (col // half) + lax.rem(col, 2)
        block = lax.rem(col, half) // 2
        small = square(units)
        flip = square(SPAN)
        for c in range(half // 2):
            place = one_hot(same & (block == c))
            at = slice(c * units, (c + 1) * units)
            for h in range(2):
                index = h * (half // 2) + c
                w2_ref[h, at, :] = dot(lu_ref[index], place).astype(jnp.bfloat16)
                down = dot_nt(small, ld_ref[index]).astype(jnp.bfloat16)
                w3t_ref[h, at, :] = dot(down, place).astype(jnp.bfloat16)
        for h in range(2):
            for r in range(size // SPAN):
                for q in range(size // SPAN):
                    at, to = slice(r * SPAN, (r + 1) * SPAN), slice(q * SPAN, (q + 1) * SPAN)
                    w2t_ref[h, to, at] = dot_nt(flip, w2_ref[h, at, to]).astype(jnp.bfloat16)
                    w3_ref[h, to, at] = dot_nt(flip, w3t_ref[h, at, to]).astype(jnp.bfloat16)

    def post(kind, k, source, target):
        pltpu.make_async_copy(source.at[k, me], target.at[k, me], recv_sem.at[kind, k]).start()

        for to in others:
            pltpu.make_async_remote_copy(
                src_ref=source.at[k, to], dst_ref=target.at[k, me],
                send_sem=send_sem.at[kind, k], recv_sem=recv_sem.at[kind, k],
                device_id=(tok, to), device_id_type=MESH,
            ).start()

    def sent(kind, k, source):
        part = source.at[k, pl.ds(0, count)]
        pltpu.make_async_copy(part, part, send_sem.at[kind, k]).wait()

    def arrived(kind, k, target):
        pltpu.make_async_copy(target.at[k], target.at[k], recv_sem.at[kind, k]).wait()

    wide = SPAN // rows

    def spread(w_ref, data, buffer, k):
        def part(r, carry):
            w = w_ref[pl.ds(pl.multiple_of(r * SPAN, SPAN), SPAN), :]
            value = dot(w, data).astype(jnp.bfloat16)
            buffer[k, pl.ds(r * wide, wide)] = value.reshape(wide, rows, CHUNK)
            return carry

        lax.fori_loop(0, w_ref.shape[0] // SPAN, part, 0)

    def stage_first(k):
        spread(w1_ref, x_ref[:, columns(k)], send_a, k)

    def stage_back(k):
        spread(w4t_ref, cot_ref[:, columns(k)], send_b, k)

    def rows_of(buffer, k, h):
        return buffer[k, :, h * half:(h + 1) * half, :].reshape(owners * half, CHUNK)

    def keep_block(acc, h, r, value):
        which = lax.rem(lax.broadcasted_iota(jnp.int32, (SPAN, 128), 0), half) // 4
        kept = value[:, 0:128]
        for p in range(1, half // 4):
            kept = jnp.where(which == p, value[:, p * 128:(p + 1) * 128], kept)
        acc[h, r * SPAN:(r + 1) * SPAN, :] += kept

    def stage_middle(k):
        arrived(0, k, got_first)
        sent(0, k, send_a)
        size = owners * half
        for h in range(2):
            given = rows_of(got_first, k, h)
            for r in range(size // SPAN):
                at = pl.ds(r * SPAN, SPAN)
                pre = dot(w2_ref[h, at, :], given)
                square = pre * pre
                t = jnp.tanh(ROOT * (pre + CUBIC * (square * pre)))
                cdf = 0.5 * (1.0 + t)
                hidden[h, at, :] = (pre * cdf).astype(jnp.bfloat16)
                slope[h, at, :] = cdf + (0.5 * ROOT) * pre * (1.0 - t * t) * (1.0 + (3.0 * CUBIC) * square)
        each = SPAN // half
        for h in range(2):
            for r in range(size // SPAN):
                value = dot(w3_ref[h, pl.ds(r * SPAN, SPAN), :], hidden[h]).astype(jnp.bfloat16)
                send_a[k, r * each:(r + 1) * each, h * half:(h + 1) * half, :] = value.reshape(each, half, CHUNK)
        post(2, k, send_a, got_mixed)

        arrived(1, k, got_back)
        sent(1, k, send_b)
        for h in range(2):
            given = rows_of(got_back, k, h)
            for r in range(size // SPAN):
                at = pl.ds(r * SPAN, SPAN)
                back = dot(w3t_ref[h, at, :], given)
                back_pre[h, at, :] = (back * slope[h, at, :]).astype(jnp.bfloat16)
        for h in range(2):
            for r in range(size // SPAN):
                value = dot(w2t_ref[h, pl.ds(r * SPAN, SPAN), :], back_pre[h]).astype(jnp.bfloat16)
                send_b[k, r * each:(r + 1) * each, h * half:(h + 1) * half, :] = value.reshape(each, half, CHUNK)
        post(3, k, send_b, got_last)

        for h in range(2):
            for r in range(size // SPAN):
                part = slice(r * each, (r + 1) * each)
                inner = slice(h * half, (h + 1) * half)
                back = got_back[k, part, inner, :].reshape(SPAN, CHUNK)
                keep_block(acc_ld, h, r, dot_nt(back, hidden[h]))
                first = got_first[k, part, inner, :].reshape(SPAN, CHUNK)
                keep_block(acc_lu, h, r, dot_nt(first, back_pre[h]))

    def apply(k, got, w_ref, into_ref):
        everything = got[k].reshape(owners * rows, CHUNK)
        into_ref[:, columns(k)] = dot(w_ref[...], everything).astype(jnp.bfloat16)

    def collect(k, got, data_ref, acc):
        data = data_ref[:, columns(k)]
        odd = lax.rem(lax.broadcasted_iota(jnp.int32, (SPAN, 128), 0), 2) == 1

        def part(r, carry):
            piece = got[k, pl.ds(r * wide, wide)].reshape(SPAN, CHUNK)
            value = dot_nt(piece, data)
            at = pl.ds(pl.multiple_of(r * SPAN, SPAN), SPAN)
            acc[at, :] += jnp.where(odd, value[:, 128:256], value[:, 0:128])
            return carry

        lax.fori_loop(0, owners * rows // SPAN, part, 0)

    def save_out(k):
        return pltpu.make_async_copy(out_ref.at[:, columns(k)], out_hbm.at[:, columns(k)], out_sem.at[0, k])

    def save_gt(k):
        return pltpu.make_async_copy(gt_ref.at[:, columns(k)], gt_hbm.at[:, columns(k)], out_sem.at[1, k])

    def stage_output(k):
        apply(k, got_mixed, w4_ref, out_ref)
        save_out(k).start()

    def stage_grad(k):
        apply(k, got_last, w1t_ref, gt_ref)
        save_gt(k).start()

    def sum_output(k):
        arrived(2, k, got_mixed)
        collect(k, got_mixed, cot_ref, acc_rd)

    def sum_grad(k):
        arrived(3, k, got_last)
        collect(k, got_last, x_ref, acc_ru)

    interleave()
    loads[0].wait()
    stage_first(0)
    loads[1].wait()
    stage_back(0)
    pl.semaphore_wait(barrier, count + 2)
    post(0, 0, send_a, got_first)
    post(1, 0, send_b, got_back)
    loads[2].wait()
    loads[3].wait()

    def ahead(k):
        stage_first(k)
        post(0, k, send_a, got_first)
        stage_back(k)
        post(1, k, send_b, got_back)

    for k in range(1, AHEAD):
        ahead(k)
    for acc in (acc_ru, acc_rd, acc_ld, acc_lu):
        acc[...] = jnp.zeros_like(acc)
    loads[4].wait()
    loads[5].wait()
    expand()
    turned()

    def step(k, carry):
        stage_middle(k)

        @pl.when(k + AHEAD < chunks)
        def _():
            ahead(k + AHEAD)

        @pl.when(k >= LAG)
        def _():
            sum_output(k - LAG)
            stage_output(k - LAG)
            sum_grad(k - LAG)
            stage_grad(k - LAG)

        return carry

    lax.fori_loop(0, chunks, step, 0)

    part = grads.shape[1] // 2
    core = lax.rem(tok, 2)
    mine = pl.ds(pl.multiple_of(core * part, part), part)
    theirs = pl.ds(pl.multiple_of(part - core * part, part), part)

    def pair(i):
        return pltpu.make_async_remote_copy(
            src_ref=grads.at[i, theirs], dst_ref=near.at[i], send_sem=sum_send.at[0, i], recv_sem=sum_recv.at[0, i],
            device_id=(core_peer, me), device_id_type=MESH,
        )

    def across(i):
        return pltpu.make_async_remote_copy(
            src_ref=own.at[i], dst_ref=far.at[i], send_sem=sum_send.at[1, i], recv_sem=sum_recv.at[1, i],
            device_id=(far_peer, me), device_id_type=MESH,
        )

    def share(i):
        return pltpu.make_async_remote_copy(
            src_ref=sums_ref.at[i, mine], dst_ref=sums_ref.at[i, mine],
            send_sem=sum_send.at[2, i], recv_sem=sum_recv.at[2, i],
            device_id=(core_peer, me), device_id_type=MESH,
        )

    def save(i):
        return pltpu.make_async_copy(sums_ref.at[i], sums_hbm.at[i], save_sem.at[i])

    def settle(i):
        share(i).wait()
        save(i).start()

    def begin(i):
        pair(i).start()

    def middle(i):
        pair(i).wait()
        own[i] = (grads[i, mine, :] + near[i]).astype(jnp.bfloat16)
        across(i).start()

    def finish(i):
        across(i).wait()
        sums_ref[i, mine, :] = own[i].astype(jnp.float32) + far[i].astype(jnp.float32)
        share(i).start()

    lane = lax.broadcasted_iota(jnp.int32, (owners, 128), 1)
    for h in range(2):
        for c in range(half // 2):
            for s in range(2):
                ld = acc_ld[h, pl.ds(2 * c + s, owners, stride=half), :]
                lu = acc_lu[h, pl.ds(2 * c + s, owners, stride=half), :]
                if c % 2 == 0:
                    both = jnp.where(lane < 64, ld, pltpu.roll(lu, 64, 1))
                else:
                    both = jnp.where(lane < 64, pltpu.roll(ld, 64, 1), lu)
                base = (h * (half // 2) + c) * 2 * owners
                grads[0, pl.ds(base + s, owners, stride=2), :] = both
    begin(0)

    size = owners * half
    last = chunks - 1
    for k in range(chunks - LAG, last):
        sum_output(k)
        stage_output(k)
        sum_grad(k)
        stage_grad(k)
    sum_output(last)
    for s in range(2):
        grads[1, s * size:(s + 1) * size, :] = acc_rd[pl.ds(s, size, stride=2), :]
    begin(1)
    middle(0)
    stage_output(last)
    middle(1)
    sum_grad(last)
    for s in range(2):
        grads[2, s * size:(s + 1) * size, :] = acc_ru[pl.ds(s, size, stride=2), :]
    begin(2)
    stage_grad(last)
    middle(2)
    finish(0)
    finish(1)
    settle(0)
    settle(1)
    finish(2)

    settle(2)
    def drain(k, carry):
        sent(2, k, send_a)
        sent(3, k, send_b)
        save_out(k).wait()
        save_gt(k).wait()
        return carry

    lax.fori_loop(0, chunks, drain, 0)
    for i in range(3):
        save(i).wait()


def finish(
    factor, out_hbm, gt_hbm, sums_hbm, out_to, gt_to, ru_to, lu_to, ld_to, rd_to,
    held, sums_ref, ru_ref, lu_ref, ld_ref, rd_ref, sem, sum_sem, turn_sem,
):
    slabs = held.shape[1]
    deep = out_hbm.shape[0] // slabs
    enter, leave = [], []
    sums = [pltpu.make_async_copy(sums_hbm.at[i], sums_ref.at[i], sum_sem.at[i]) for i in range(3)]
    for p in range(slabs):
        at = pl.ds(p * deep, deep)
        for i, (source, target) in enumerate(((out_hbm, out_to), (gt_hbm, gt_to))):
            enter.append(pltpu.make_async_copy(source.at[at], held.at[i, p], sem.at[0, i, p]))
            leave.append(pltpu.make_async_copy(held.at[i, p], target.at[at], sem.at[1, i, p]))
    for copy in enter[:2] + sums + enter[2:]:
        copy.start()
    turned = [
        pltpu.make_async_copy(source, target, turn_sem.at[i])
        for i, (source, target) in enumerate(((ld_ref, ld_to), (lu_ref, lu_to), (rd_ref, rd_to), (ru_ref, ru_to)))
    ]

    def forward(part):
        for i in part:
            enter[i].wait()
            leave[i].start()

    units = ld_ref.shape[1]
    size = sums_ref.shape[1] // 2
    forward(range(0, 2))
    sums[0].wait()
    for c in range(ld_ref.shape[0]):
        both = sums_ref[0, c * units:(c + 1) * units, :] * factor
        ld_ref[c] = both[:, :units]
        lu_ref[c] = both.T[units:, :]
    turned[0].start()
    turned[1].start()
    forward(range(2, 4))
    sums[1].wait()
    for s in range(2):
        rd_ref[s] = (sums_ref[1, s * size:(s + 1) * size, :] * factor).T
    turned[2].start()
    forward(range(4, 6))
    sums[2].wait()
    for s in range(2):
        ru_ref[s] = sums_ref[2, s * size:(s + 1) * size, :] * factor
    turned[3].start()
    forward(range(6, 2 * slabs))
    for copy in leave + turned:
        copy.wait()


def shards(tokens, cotangent, right_up, left_up, left_down, right_down):
    tok_count = lax.axis_size("tok")
    owners = lax.axis_size("blk")
    factor = float(tokens.shape[2] * tok_count) ** (-0.5)
    pair, width, count = tokens.shape
    hidden_blocks = right_up.shape[1]
    own_blocks = left_up.shape[0]
    units = left_up.shape[1]
    eight = own_blocks // 2
    chunks = count // CHUNK
    bf = jnp.bfloat16

    wide, deep = pair * hidden_blocks, pair * width
    size = eight * units
    rows = pair * own_blocks
    flow = pltpu.VMEM((chunks, owners, rows, CHUNK), bf)
    vmem = pl.BlockSpec(memory_space=pltpu.VMEM)
    hbm = pl.BlockSpec(memory_space=pltpu.HBM)
    output, grad_tokens, sums = pl.pallas_call(
        functools.partial(kernel, chunks, owners),
        out_shape=(
            jax.ShapeDtypeStruct((deep, count), bf),
            jax.ShapeDtypeStruct((deep, count), bf),
            jax.ShapeDtypeStruct((3, wide, 128), jnp.float32),
        ),
        in_specs=[hbm, hbm, vmem, vmem, hbm, hbm],
        out_specs=(hbm, hbm, hbm),
        scratch_shapes=[
            pltpu.VMEM((deep, count), bf), pltpu.VMEM((deep, count), bf),
            pltpu.VMEM(left_up.shape, bf), pltpu.VMEM(left_down.shape, bf),
            pltpu.VMEM((deep, count), bf), pltpu.VMEM((deep, count), bf),
            pltpu.VMEM((wide, deep), bf), pltpu.VMEM((deep, wide), bf),
            pltpu.VMEM((2, size, size), bf), pltpu.VMEM((2, size, size), bf),
            pltpu.VMEM((2, size, size), bf), pltpu.VMEM((2, size, size), bf),
            pltpu.VMEM((deep, wide), bf), pltpu.VMEM((wide, deep), bf),
            flow, flow, flow, flow, flow, flow,
            pltpu.VMEM((2, size, CHUNK), bf),
            pltpu.VMEM((2, size, CHUNK), jnp.float32),
            pltpu.VMEM((2, size, CHUNK), bf),
            pltpu.VMEM((wide, 128), jnp.float32),
            pltpu.VMEM((wide, 128), jnp.float32),
            pltpu.VMEM((2, size, 128), jnp.float32),
            pltpu.VMEM((2, size, 128), jnp.float32),
            pltpu.VMEM((3, wide, 128), jnp.float32),
            pltpu.VMEM((3, wide // 2, 128), jnp.float32),
            pltpu.VMEM((3, wide // 2, 128), bf),
            pltpu.VMEM((3, wide // 2, 128), bf),
            pltpu.VMEM((3, wide, 128), jnp.float32),
            pltpu.SemaphoreType.DMA((4, chunks)),
            pltpu.SemaphoreType.DMA((4, chunks)),
            pltpu.SemaphoreType.DMA((3, 3)),
            pltpu.SemaphoreType.DMA((3, 3)),
            pltpu.SemaphoreType.DMA((6,)),
            pltpu.SemaphoreType.DMA((2, chunks)),
            pltpu.SemaphoreType.DMA((3,)),
        ],
        compiler_params=pltpu.CompilerParams(
            collective_id=0, has_side_effects=True, vmem_limit_bytes=60 << 20
        ),
        name="monarch",
    )(
        tokens.reshape(deep, count), cotangent.reshape(deep, count),
        right_up, right_down, left_up, left_down,
    )
    shape = tokens.shape
    output, grad_tokens, grad_ru, grad_lu, grad_ld, grad_rd = pl.pallas_call(
        functools.partial(finish, factor),
        out_shape=(
            jax.ShapeDtypeStruct((deep, count), bf),
            jax.ShapeDtypeStruct((deep, count), bf),
            jax.ShapeDtypeStruct(right_up.shape, jnp.float32),
            jax.ShapeDtypeStruct(left_up.shape, jnp.float32),
            jax.ShapeDtypeStruct(left_down.shape, jnp.float32),
            jax.ShapeDtypeStruct(right_down.shape, jnp.float32),
        ),
        in_specs=[hbm, hbm, hbm],
        out_specs=(hbm,) * 6,
        scratch_shapes=[
            pltpu.VMEM((2, 4, deep // 4, count), bf),
            pltpu.VMEM((3, wide, 128), jnp.float32),
            pltpu.VMEM(right_up.shape, jnp.float32), pltpu.VMEM(left_up.shape, jnp.float32),
            pltpu.VMEM(left_down.shape, jnp.float32), pltpu.VMEM(right_down.shape, jnp.float32),
            pltpu.SemaphoreType.DMA((2, 2, 4)), pltpu.SemaphoreType.DMA((3,)), pltpu.SemaphoreType.DMA((4,)),
        ],
        compiler_params=pltpu.CompilerParams(vmem_limit_bytes=60 << 20),
        name="finish",
    )(output, grad_tokens, sums)
    return (output.reshape(shape), grad_tokens.reshape(shape), grad_ru, grad_lu, grad_ld, grad_rd)


def solution(mesh):
    split = P("blk", None, "tok")
    whole = P("blk", None, None)
    return jax.shard_map(
        shards,
        mesh=mesh,
        in_specs=(split, split, whole, whole, whole, whole),
        out_specs=(split, split, whole, whole, whole, whole),
        check_vma=False,
    )
```

```python
import functools

import jax
import jax.numpy as jnp
from jax import lax
from jax.experimental import pallas as pl
from jax.experimental.pallas import tpu as pltpu
from jax.sharding import PartitionSpec as P

MESH = pl.DeviceIdType.MESH
CHUNK = 256
AHEAD = 4
LAG = 2
SPAN = 256
ROOT = 0.7978845608028654
CUBIC = 0.044715


def dot(a, b):
    return jnp.dot(a, b, preferred_element_type=jnp.float32)


def dot_nt(a, b):
    return lax.dot_general(a, b, (((1,), (1,)), ((), ())), preferred_element_type=jnp.float32)


def hops():
    near = lambda v: min(v, 4 - v)
    steps = [(x, z, y) for x in range(4) for z in range(4) for y in range(2)][1:]
    order = []
    for step in sorted(steps, key=lambda s: -(near(s[0]) + near(s[1]) + s[2])):
        for x, z in ((step[0], step[1]), (step[1], step[0])):
            for twin in ((x, z, step[2]), (-x % 4, -z % 4, step[2])):
                if twin not in order:
                    order.append(twin)
    return order


def neighbour(me, step):
    x, z, y = me // 8, lax.rem(me // 2, 4), lax.rem(me, 2)
    return (lax.rem(x + step[0], 4) * 4 + lax.rem(z + step[1], 4)) * 2 + lax.rem(y + step[2], 2)


def one_hot(test):
    return jnp.where(test, 1.0, 0.0).astype(jnp.bfloat16)


def square(size):
    row = lax.broadcasted_iota(jnp.int32, (size, size), 0)
    return one_hot(row == lax.broadcasted_iota(jnp.int32, (size, size), 1))


def kernel(
    chunks, owners, x_hbm, cot_hbm, ru_ref, rd_ref, lu_hbm, ld_hbm,
    out_hbm, gt_hbm, sums_hbm,
    x_ref, cot_ref, lu_ref, ld_ref, out_ref, gt_ref,
    w1_ref, w1t_ref, w2_ref, w2t_ref, w3_ref, w3t_ref, w4_ref, w4t_ref,
    send_a, send_b, got_first, got_back, got_mixed, got_last, hidden, slope, back_pre,
    acc_ru, acc_rd, acc_ld, acc_lu, grads, near, own, far, sums_ref,
    send_sem, recv_sem, sum_send, sum_recv, in_sem, out_sem, save_sem,
):
    me = lax.axis_index("blk")
    tok = lax.axis_index("tok")
    core_peer = tok + 1 - 2 * lax.rem(tok, 2)
    far_peer = tok + 2 - 4 * (tok // 2)
    rows = send_a.shape[2]
    half = rows // 2
    count = owners - 1
    others = [neighbour(me, step) for step in hops()]

    def columns(k):
        return pl.ds(pl.multiple_of(k * CHUNK, CHUNK), CHUNK)

    head, tail = pl.ds(0, CHUNK), pl.ds(CHUNK, x_ref.shape[1] - CHUNK)
    loads = [
        pltpu.make_async_copy(x_hbm.at[:, head], x_ref.at[:, head], in_sem.at[0]),
        pltpu.make_async_copy(cot_hbm.at[:, head], cot_ref.at[:, head], in_sem.at[1]),
        pltpu.make_async_copy(x_hbm.at[:, tail], x_ref.at[:, tail], in_sem.at[2]),
        pltpu.make_async_copy(cot_hbm.at[:, tail], cot_ref.at[:, tail], in_sem.at[3]),
        pltpu.make_async_copy(lu_hbm, lu_ref, in_sem.at[4]),
        pltpu.make_async_copy(ld_hbm, ld_ref, in_sem.at[5]),
    ]
    for load in loads:
        load.start()

    barrier = pltpu.get_barrier_semaphore()

    for to in others:
        pl.semaphore_signal(barrier, inc=1, device_id=(tok, to), device_id_type=MESH)
    pl.semaphore_signal(barrier, inc=1, device_id=(core_peer, me), device_id_type=MESH)
    pl.semaphore_signal(barrier, inc=1, device_id=(far_peer, me), device_id_type=MESH)

    def interleave():
        row = lax.broadcasted_iota(jnp.int32, (SPAN, SPAN // 2), 0)
        spot = 2 * lax.broadcasted_iota(jnp.int32, (SPAN, SPAN // 2), 1)
        for s in range(2):
            pick = one_hot(row == spot + s)
            for r in range(w1_ref.shape[0] // SPAN):
                at, part = slice(r * SPAN, (r + 1) * SPAN), slice(r * SPAN // 2, (r + 1) * SPAN // 2)
                lanes = slice(s * 128, (s + 1) * 128)
                w1_ref[at, lanes] = dot(pick, ru_ref[s, part, :]).astype(jnp.bfloat16)
                w4t_ref[at, lanes] = dot_nt(pick, rd_ref[s, :, part]).astype(jnp.bfloat16)

    def turned():
        flip = square(SPAN)
        for r in range(w1_ref.shape[0] // SPAN):
            at = slice(r * SPAN, (r + 1) * SPAN)
            w1t_ref[:, at] = dot_nt(flip, w1_ref[at, :]).astype(jnp.bfloat16)
            w4_ref[:, at] = dot_nt(flip, w4t_ref[at, :]).astype(jnp.bfloat16)

    def expand():
        units = lu_ref.shape[1]
        size = owners * half
        row = lax.broadcasted_iota(jnp.int32, (units, size), 0)
        col = lax.broadcasted_iota(jnp.int32, (units, size), 1)
        same = row == 2 * (col // half) + lax.rem(col, 2)
        block = lax.rem(col, half) // 2
        small = square(units)
        flip = square(SPAN)
        for c in range(half // 2):
            place = one_hot(same & (block == c))
            at = slice(c * units, (c + 1) * units)
            for h in range(2):
                index = h * (half // 2) + c
                w2_ref[h, at, :] = dot(lu_ref[index], place).astype(jnp.bfloat16)
                down = dot_nt(small, ld_ref[index]).astype(jnp.bfloat16)
                w3t_ref[h, at, :] = dot(down, place).astype(jnp.bfloat16)
        for h in range(2):
            for r in range(size // SPAN):
                for q in range(size // SPAN):
                    at, to = slice(r * SPAN, (r + 1) * SPAN), slice(q * SPAN, (q + 1) * SPAN)
                    w2t_ref[h, to, at] = dot_nt(flip, w2_ref[h, at, to]).astype(jnp.bfloat16)
                    w3_ref[h, to, at] = dot_nt(flip, w3t_ref[h, at, to]).astype(jnp.bfloat16)

    def post(kind, k, source, target):
        pltpu.make_async_copy(source.at[k, me], target.at[k, me], recv_sem.at[kind, k]).start()

        for to in others:
            pltpu.make_async_remote_copy(
                src_ref=source.at[k, to], dst_ref=target.at[k, me],
                send_sem=send_sem.at[kind, k], recv_sem=recv_sem.at[kind, k],
                device_id=(tok, to), device_id_type=MESH,
            ).start()

    def sent(kind, k, source):
        part = source.at[k, pl.ds(0, count)]
        pltpu.make_async_copy(part, part, send_sem.at[kind, k]).wait()

    def arrived(kind, k, target):
        pltpu.make_async_copy(target.at[k], target.at[k], recv_sem.at[kind, k]).wait()

    wide = SPAN // rows

    def spread(w_ref, data, buffer, k):
        def part(r, carry):
            w = w_ref[pl.ds(pl.multiple_of(r * SPAN, SPAN), SPAN), :]
            value = dot(w, data).astype(jnp.bfloat16)
            buffer[k, pl.ds(r * wide, wide)] = value.reshape(wide, rows, CHUNK)
            return carry

        lax.fori_loop(0, w_ref.shape[0] // SPAN, part, 0)

    def stage_first(k):
        spread(w1_ref, x_ref[:, columns(k)], send_a, k)

    def stage_back(k):
        spread(w4t_ref, cot_ref[:, columns(k)], send_b, k)

    def rows_of(buffer, k, h):
        return buffer[k, :, h * half:(h + 1) * half, :].reshape(owners * half, CHUNK)

    def keep_block(acc, h, r, value):
        which = lax.rem(lax.broadcasted_iota(jnp.int32, (SPAN, 128), 0), half) // 4
        kept = value[:, 0:128]
        for p in range(1, half // 4):
            kept = jnp.where(which == p, value[:, p * 128:(p + 1) * 128], kept)
        acc[h, r * SPAN:(r + 1) * SPAN, :] += kept

    def stage_middle(k):
        arrived(0, k, got_first)
        sent(0, k, send_a)
        size = owners * half
        for h in range(2):
            given = rows_of(got_first, k, h)
            for r in range(size // SPAN):
                at = pl.ds(r * SPAN, SPAN)
                pre = dot(w2_ref[h, at, :], given)
                square = pre * pre
                t = jnp.tanh(ROOT * (pre + CUBIC * (square * pre)))
                cdf = 0.5 * (1.0 + t)
                hidden[h, at, :] = (pre * cdf).astype(jnp.bfloat16)
                slope[h, at, :] = cdf + (0.5 * ROOT) * pre * (1.0 - t * t) * (1.0 + (3.0 * CUBIC) * square)
        each = SPAN // half
        for h in range(2):
            for r in range(size // SPAN):
                value = dot(w3_ref[h, pl.ds(r * SPAN, SPAN), :], hidden[h]).astype(jnp.bfloat16)
                send_a[k, r * each:(r + 1) * each, h * half:(h + 1) * half, :] = value.reshape(each, half, CHUNK)
        post(2, k, send_a, got_mixed)

        arrived(1, k, got_back)
        sent(1, k, send_b)
        for h in range(2):
            given = rows_of(got_back, k, h)
            for r in range(size // SPAN):
                at = pl.ds(r * SPAN, SPAN)
                back = dot(w3t_ref[h, at, :], given)
                back_pre[h, at, :] = (back * slope[h, at, :]).astype(jnp.bfloat16)
        for h in range(2):
            for r in range(size // SPAN):
                value = dot(w2t_ref[h, pl.ds(r * SPAN, SPAN), :], back_pre[h]).astype(jnp.bfloat16)
                send_b[k, r * each:(r + 1) * each, h * half:(h + 1) * half, :] = value.reshape(each, half, CHUNK)
        post(3, k, send_b, got_last)

        for h in range(2):
            for r in range(size // SPAN):
                part = slice(r * each, (r + 1) * each)
                inner = slice(h * half, (h + 1) * half)
                back = got_back[k, part, inner, :].reshape(SPAN, CHUNK)
                keep_block(acc_ld, h, r, dot_nt(back, hidden[h]))
                first = got_first[k, part, inner, :].reshape(SPAN, CHUNK)
                keep_block(acc_lu, h, r, dot_nt(first, back_pre[h]))

    def apply(k, got, w_ref, into_ref):
        everything = got[k].reshape(owners * rows, CHUNK)
        into_ref[:, columns(k)] = dot(w_ref[...], everything).astype(jnp.bfloat16)

    def collect(k, got, data_ref, acc):
        data = data_ref[:, columns(k)]
        odd = lax.rem(lax.broadcasted_iota(jnp.int32, (SPAN, 128), 0), 2) == 1

        def part(r, carry):
            piece = got[k, pl.ds(r * wide, wide)].reshape(SPAN, CHUNK)
            value = dot_nt(piece, data)
            at = pl.ds(pl.multiple_of(r * SPAN, SPAN), SPAN)
            acc[at, :] += jnp.where(odd, value[:, 128:256], value[:, 0:128])
            return carry

        lax.fori_loop(0, owners * rows // SPAN, part, 0)

    def save_out(k):
        return pltpu.make_async_copy(out_ref.at[:, columns(k)], out_hbm.at[:, columns(k)], out_sem.at[0, k])

    def save_gt(k):
        return pltpu.make_async_copy(gt_ref.at[:, columns(k)], gt_hbm.at[:, columns(k)], out_sem.at[1, k])

    def stage_output(k):
        apply(k, got_mixed, w4_ref, out_ref)
        save_out(k).start()

    def stage_grad(k):
        apply(k, got_last, w1t_ref, gt_ref)
        save_gt(k).start()

    def sum_output(k):
        arrived(2, k, got_mixed)
        collect(k, got_mixed, cot_ref, acc_rd)

    def sum_grad(k):
        arrived(3, k, got_last)
        collect(k, got_last, x_ref, acc_ru)

    interleave()
    loads[0].wait()
    stage_first(0)
    loads[1].wait()
    stage_back(0)
    pl.semaphore_wait(barrier, count + 2)
    post(0, 0, send_a, got_first)
    post(1, 0, send_b, got_back)
    loads[2].wait()
    loads[3].wait()

    def ahead(k):
        stage_first(k)
        post(0, k, send_a, got_first)
        stage_back(k)
        post(1, k, send_b, got_back)

    for k in range(1, AHEAD):
        ahead(k)
    for acc in (acc_ru, acc_rd, acc_ld, acc_lu):
        acc[...] = jnp.zeros_like(acc)
    loads[4].wait()
    loads[5].wait()
    expand()
    turned()

    def step(k, carry):
        stage_middle(k)

        @pl.when(k + AHEAD < chunks)
        def _():
            ahead(k + AHEAD)

        @pl.when(k >= LAG)
        def _():
            sum_output(k - LAG)
            stage_output(k - LAG)
            sum_grad(k - LAG)
            stage_grad(k - LAG)

        return carry

    lax.fori_loop(0, chunks, step, 0)

    part = grads.shape[1] // 2
    core = lax.rem(tok, 2)
    mine = pl.ds(pl.multiple_of(core * part, part), part)
    theirs = pl.ds(pl.multiple_of(part - core * part, part), part)

    def pair(i):
        return pltpu.make_async_remote_copy(
            src_ref=grads.at[i, theirs], dst_ref=near.at[i], send_sem=sum_send.at[0, i], recv_sem=sum_recv.at[0, i],
            device_id=(core_peer, me), device_id_type=MESH,
        )

    def across(i):
        return pltpu.make_async_remote_copy(
            src_ref=own.at[i], dst_ref=far.at[i], send_sem=sum_send.at[1, i], recv_sem=sum_recv.at[1, i],
            device_id=(far_peer, me), device_id_type=MESH,
        )

    def share(i):
        return pltpu.make_async_remote_copy(
            src_ref=sums_ref.at[i], dst_ref=sums_hbm.at[i, mine],
            send_sem=sum_send.at[2, i], recv_sem=sum_recv.at[2, i],
            device_id=(core_peer, me), device_id_type=MESH,
        )

    def save(i):
        return pltpu.make_async_copy(sums_ref.at[i], sums_hbm.at[i, mine], save_sem.at[i])

    def begin(i):
        pair(i).start()

    def middle(i):
        pair(i).wait()
        own[i] = (grads[i, mine, :] + near[i]).astype(jnp.bfloat16)
        across(i).start()

    def finish(i):
        across(i).wait()
        sums_ref[i] = own[i].astype(jnp.float32) + far[i].astype(jnp.float32)
        share(i).start()
        save(i).start()

    lane = lax.broadcasted_iota(jnp.int32, (owners, 128), 1)
    for h in range(2):
        for c in range(half // 2):
            for s in range(2):
                ld = acc_ld[h, pl.ds(2 * c + s, owners, stride=half), :]
                lu = acc_lu[h, pl.ds(2 * c + s, owners, stride=half), :]
                if c % 2 == 0:
                    both = jnp.where(lane < 64, ld, pltpu.roll(lu, 64, 1))
                else:
                    both = jnp.where(lane < 64, pltpu.roll(ld, 64, 1), lu)
                base = (h * (half // 2) + c) * 2 * owners
                grads[0, pl.ds(base + s, owners, stride=2), :] = both
    begin(0)

    size = owners * half
    last = chunks - 1
    for k in range(chunks - LAG, last):
        sum_output(k)
        stage_output(k)
        sum_grad(k)
        stage_grad(k)
    sum_output(last)
    for s in range(2):
        grads[1, s * size:(s + 1) * size, :] = acc_rd[pl.ds(s, size, stride=2), :]
    begin(1)
    middle(0)
    stage_output(last)
    middle(1)
    sum_grad(last)
    for s in range(2):
        grads[2, s * size:(s + 1) * size, :] = acc_ru[pl.ds(s, size, stride=2), :]
    begin(2)
    stage_grad(last)
    middle(2)
    finish(0)
    finish(1)
    finish(2)

    def drain(k, carry):
        sent(2, k, send_a)
        sent(3, k, send_b)
        save_out(k).wait()
        save_gt(k).wait()
        return carry

    lax.fori_loop(0, chunks, drain, 0)
    for i in range(3):
        share(i).wait()
        save(i).wait()


def finish(
    factor, out_hbm, gt_hbm, sums_hbm, out_to, gt_to, ru_to, lu_to, ld_to, rd_to,
    held, sums_ref, ru_ref, lu_ref, ld_ref, rd_ref, sem, sum_sem, turn_sem,
):
    slabs = held.shape[1]
    deep = out_hbm.shape[0] // slabs
    enter, leave = [], []
    sums = [pltpu.make_async_copy(sums_hbm.at[i], sums_ref.at[i], sum_sem.at[i]) for i in range(3)]
    for p in range(slabs):
        at = pl.ds(p * deep, deep)
        for i, (source, target) in enumerate(((out_hbm, out_to), (gt_hbm, gt_to))):
            enter.append(pltpu.make_async_copy(source.at[at], held.at[i, p], sem.at[0, i, p]))
            leave.append(pltpu.make_async_copy(held.at[i, p], target.at[at], sem.at[1, i, p]))
    for copy in enter[:2] + sums + enter[2:]:
        copy.start()
    turned = [
        pltpu.make_async_copy(source, target, turn_sem.at[i])
        for i, (source, target) in enumerate(((ld_ref, ld_to), (lu_ref, lu_to), (rd_ref, rd_to), (ru_ref, ru_to)))
    ]

    def forward(part):
        for i in part:
            enter[i].wait()
            leave[i].start()

    units = ld_ref.shape[1]
    size = sums_ref.shape[1] // 2
    forward(range(0, 2))
    sums[0].wait()
    for c in range(ld_ref.shape[0]):
        both = sums_ref[0, c * units:(c + 1) * units, :] * factor
        ld_ref[c] = both[:, :units]
        lu_ref[c] = both.T[units:, :]
    turned[0].start()
    turned[1].start()
    forward(range(2, 4))
    sums[1].wait()
    for s in range(2):
        rd_ref[s] = (sums_ref[1, s * size:(s + 1) * size, :] * factor).T
    turned[2].start()
    forward(range(4, 6))
    sums[2].wait()
    for s in range(2):
        ru_ref[s] = sums_ref[2, s * size:(s + 1) * size, :] * factor
    turned[3].start()
    forward(range(6, 2 * slabs))
    for copy in leave + turned:
        copy.wait()


def shards(tokens, cotangent, right_up, left_up, left_down, right_down):
    tok_count = lax.axis_size("tok")
    owners = lax.axis_size("blk")
    factor = float(tokens.shape[2] * tok_count) ** (-0.5)
    pair, width, count = tokens.shape
    hidden_blocks = right_up.shape[1]
    own_blocks = left_up.shape[0]
    units = left_up.shape[1]
    eight = own_blocks // 2
    chunks = count // CHUNK
    bf = jnp.bfloat16

    wide, deep = pair * hidden_blocks, pair * width
    size = eight * units
    rows = pair * own_blocks
    flow = pltpu.VMEM((chunks, owners, rows, CHUNK), bf)
    vmem = pl.BlockSpec(memory_space=pltpu.VMEM)
    hbm = pl.BlockSpec(memory_space=pltpu.HBM)
    output, grad_tokens, sums = pl.pallas_call(
        functools.partial(kernel, chunks, owners),
        out_shape=(
            jax.ShapeDtypeStruct((deep, count), bf),
            jax.ShapeDtypeStruct((deep, count), bf),
            jax.ShapeDtypeStruct((3, wide, 128), jnp.float32),
        ),
        in_specs=[hbm, hbm, vmem, vmem, hbm, hbm],
        out_specs=(hbm, hbm, hbm),
        scratch_shapes=[
            pltpu.VMEM((deep, count), bf), pltpu.VMEM((deep, count), bf),
            pltpu.VMEM(left_up.shape, bf), pltpu.VMEM(left_down.shape, bf),
            pltpu.VMEM((deep, count), bf), pltpu.VMEM((deep, count), bf),
            pltpu.VMEM((wide, deep), bf), pltpu.VMEM((deep, wide), bf),
            pltpu.VMEM((2, size, size), bf), pltpu.VMEM((2, size, size), bf),
            pltpu.VMEM((2, size, size), bf), pltpu.VMEM((2, size, size), bf),
            pltpu.VMEM((deep, wide), bf), pltpu.VMEM((wide, deep), bf),
            flow, flow, flow, flow, flow, flow,
            pltpu.VMEM((2, size, CHUNK), bf),
            pltpu.VMEM((2, size, CHUNK), jnp.float32),
            pltpu.VMEM((2, size, CHUNK), bf),
            pltpu.VMEM((wide, 128), jnp.float32),
            pltpu.VMEM((wide, 128), jnp.float32),
            pltpu.VMEM((2, size, 128), jnp.float32),
            pltpu.VMEM((2, size, 128), jnp.float32),
            pltpu.VMEM((3, wide, 128), jnp.float32),
            pltpu.VMEM((3, wide // 2, 128), jnp.float32),
            pltpu.VMEM((3, wide // 2, 128), bf),
            pltpu.VMEM((3, wide // 2, 128), bf),
            pltpu.VMEM((3, wide // 2, 128), jnp.float32),
            pltpu.SemaphoreType.DMA((4, chunks)),
            pltpu.SemaphoreType.DMA((4, chunks)),
            pltpu.SemaphoreType.DMA((3, 3)),
            pltpu.SemaphoreType.DMA((3, 3)),
            pltpu.SemaphoreType.DMA((6,)),
            pltpu.SemaphoreType.DMA((2, chunks)),
            pltpu.SemaphoreType.DMA((3,)),
        ],
        compiler_params=pltpu.CompilerParams(
            collective_id=0, has_side_effects=True, vmem_limit_bytes=60 << 20
        ),
        name="monarch",
    )(
        tokens.reshape(deep, count), cotangent.reshape(deep, count),
        right_up, right_down, left_up, left_down,
    )
    shape = tokens.shape
    output, grad_tokens, grad_ru, grad_lu, grad_ld, grad_rd = pl.pallas_call(
        functools.partial(finish, factor),
        out_shape=(
            jax.ShapeDtypeStruct((deep, count), bf),
            jax.ShapeDtypeStruct((deep, count), bf),
            jax.ShapeDtypeStruct(right_up.shape, jnp.float32),
            jax.ShapeDtypeStruct(left_up.shape, jnp.float32),
            jax.ShapeDtypeStruct(left_down.shape, jnp.float32),
            jax.ShapeDtypeStruct(right_down.shape, jnp.float32),
        ),
        in_specs=[hbm, hbm, hbm],
        out_specs=(hbm,) * 6,
        scratch_shapes=[
            pltpu.VMEM((2, 4, deep // 4, count), bf),
            pltpu.VMEM((3, wide, 128), jnp.float32),
            pltpu.VMEM(right_up.shape, jnp.float32), pltpu.VMEM(left_up.shape, jnp.float32),
            pltpu.VMEM(left_down.shape, jnp.float32), pltpu.VMEM(right_down.shape, jnp.float32),
            pltpu.SemaphoreType.DMA((2, 2, 4)), pltpu.SemaphoreType.DMA((3,)), pltpu.SemaphoreType.DMA((4,)),
        ],
        compiler_params=pltpu.CompilerParams(vmem_limit_bytes=60 << 20),
        name="finish",
    )(output, grad_tokens, sums)
    return (output.reshape(shape), grad_tokens.reshape(shape), grad_ru, grad_lu, grad_ld, grad_rd)


def solution(mesh):
    split = P("blk", None, "tok")
    whole = P("blk", None, None)
    return jax.shard_map(
        shards,
        mesh=mesh,
        in_specs=(split, split, whole, whole, whole, whole),
        out_specs=(split, split, whole, whole, whole, whole),
        check_vma=False,
    )
```

```python
import functools

import jax
import jax.numpy as jnp
from jax import lax
from jax.experimental import pallas as pl
from jax.experimental.pallas import tpu as pltpu
from jax.sharding import PartitionSpec as P

MESH = pl.DeviceIdType.MESH
CHUNK = 512
AHEAD = 2
LAG = 1
SPAN = 256
ROOT = 0.7978845608028654
CUBIC = 0.044715


def dot(a, b):
    return jnp.dot(a, b, preferred_element_type=jnp.float32)


def dot_nt(a, b):
    return lax.dot_general(a, b, (((1,), (1,)), ((), ())), preferred_element_type=jnp.float32)


def hops():
    near = lambda v: min(v, 4 - v)
    steps = [(x, z, y) for x in range(4) for z in range(4) for y in range(2)][1:]
    order = []
    for step in sorted(steps, key=lambda s: -(near(s[0]) + near(s[1]) + s[2])):
        for x, z in ((step[0], step[1]), (step[1], step[0])):
            for twin in ((x, z, step[2]), (-x % 4, -z % 4, step[2])):
                if twin not in order:
                    order.append(twin)
    return order


def neighbour(me, step):
    x, z, y = me // 8, lax.rem(me // 2, 4), lax.rem(me, 2)
    return (lax.rem(x + step[0], 4) * 4 + lax.rem(z + step[1], 4)) * 2 + lax.rem(y + step[2], 2)


def one_hot(test):
    return jnp.where(test, 1.0, 0.0).astype(jnp.bfloat16)


def square(size):
    row = lax.broadcasted_iota(jnp.int32, (size, size), 0)
    return one_hot(row == lax.broadcasted_iota(jnp.int32, (size, size), 1))


def kernel(
    chunks, owners, x_hbm, cot_hbm, ru_ref, rd_ref, lu_hbm, ld_hbm,
    out_hbm, gt_hbm, sums_hbm,
    x_ref, cot_ref, lu_ref, ld_ref, out_ref, gt_ref,
    w1_ref, w1t_ref, w2_ref, w2t_ref, w3_ref, w3t_ref, w4_ref, w4t_ref,
    send_a, send_b, got_first, got_back, got_mixed, got_last, hidden, slope, back_pre,
    acc_ru, acc_rd, acc_ld, acc_lu, grads, near, own, far, sums_ref,
    send_sem, recv_sem, sum_send, sum_recv, in_sem, out_sem, save_sem,
):
    me = lax.axis_index("blk")
    tok = lax.axis_index("tok")
    core_peer = tok + 1 - 2 * lax.rem(tok, 2)
    far_peer = tok + 2 - 4 * (tok // 2)
    rows = send_a.shape[2]
    half = rows // 2
    count = owners - 1
    others = [neighbour(me, step) for step in hops()]

    def columns(k):
        return pl.ds(pl.multiple_of(k * CHUNK, CHUNK), CHUNK)

    head, tail = pl.ds(0, CHUNK), pl.ds(CHUNK, x_ref.shape[1] - CHUNK)
    loads = [
        pltpu.make_async_copy(x_hbm.at[:, head], x_ref.at[:, head], in_sem.at[0]),
        pltpu.make_async_copy(cot_hbm.at[:, head], cot_ref.at[:, head], in_sem.at[1]),
        pltpu.make_async_copy(x_hbm.at[:, tail], x_ref.at[:, tail], in_sem.at[2]),
        pltpu.make_async_copy(cot_hbm.at[:, tail], cot_ref.at[:, tail], in_sem.at[3]),
        pltpu.make_async_copy(lu_hbm, lu_ref, in_sem.at[4]),
        pltpu.make_async_copy(ld_hbm, ld_ref, in_sem.at[5]),
    ]
    for load in loads:
        load.start()

    barrier = pltpu.get_barrier_semaphore()

    for to in others:
        pl.semaphore_signal(barrier, inc=1, device_id=(tok, to), device_id_type=MESH)
    pl.semaphore_signal(barrier, inc=1, device_id=(core_peer, me), device_id_type=MESH)
    pl.semaphore_signal(barrier, inc=1, device_id=(far_peer, me), device_id_type=MESH)

    def interleave():
        row = lax.broadcasted_iota(jnp.int32, (SPAN, SPAN // 2), 0)
        spot = 2 * lax.broadcasted_iota(jnp.int32, (SPAN, SPAN // 2), 1)
        for s in range(2):
            pick = one_hot(row == spot + s)
            for r in range(w1_ref.shape[0] // SPAN):
                at, part = slice(r * SPAN, (r + 1) * SPAN), slice(r * SPAN // 2, (r + 1) * SPAN // 2)
                lanes = slice(s * 128, (s + 1) * 128)
                w1_ref[at, lanes] = dot(pick, ru_ref[s, part, :]).astype(jnp.bfloat16)
                w4t_ref[at, lanes] = dot_nt(pick, rd_ref[s, :, part]).astype(jnp.bfloat16)

    def turned():
        flip = square(SPAN)
        for r in range(w1_ref.shape[0] // SPAN):
            at = slice(r * SPAN, (r + 1) * SPAN)
            w1t_ref[:, at] = dot_nt(flip, w1_ref[at, :]).astype(jnp.bfloat16)
            w4_ref[:, at] = dot_nt(flip, w4t_ref[at, :]).astype(jnp.bfloat16)

    def expand():
        units = lu_ref.shape[1]
        size = owners * half
        row = lax.broadcasted_iota(jnp.int32, (units, size), 0)
        col = lax.broadcasted_iota(jnp.int32, (units, size), 1)
        same = row == 2 * (col // half) + lax.rem(col, 2)
        block = lax.rem(col, half) // 2
        small = square(units)
        flip = square(SPAN)
        for c in range(half // 2):
            place = one_hot(same & (block == c))
            at = slice(c * units, (c + 1) * units)
            for h in range(2):
                index = h * (half // 2) + c
                w2_ref[h, at, :] = dot(lu_ref[index], place).astype(jnp.bfloat16)
                down = dot_nt(small, ld_ref[index]).astype(jnp.bfloat16)
                w3t_ref[h, at, :] = dot(down, place).astype(jnp.bfloat16)
        for h in range(2):
            for r in range(size // SPAN):
                for q in range(size // SPAN):
                    at, to = slice(r * SPAN, (r + 1) * SPAN), slice(q * SPAN, (q + 1) * SPAN)
                    w2t_ref[h, to, at] = dot_nt(flip, w2_ref[h, at, to]).astype(jnp.bfloat16)
                    w3_ref[h, to, at] = dot_nt(flip, w3t_ref[h, at, to]).astype(jnp.bfloat16)

    def post(kind, k, source, target):
        pltpu.make_async_copy(source.at[k, me], target.at[k, me], recv_sem.at[kind, k]).start()

        for to in others:
            pltpu.make_async_remote_copy(
                src_ref=source.at[k, to], dst_ref=target.at[k, me],
                send_sem=send_sem.at[kind, k], recv_sem=recv_sem.at[kind, k],
                device_id=(tok, to), device_id_type=MESH,
            ).start()

    def sent(kind, k, source):
        part = source.at[k, pl.ds(0, count)]
        pltpu.make_async_copy(part, part, send_sem.at[kind, k]).wait()

    def arrived(kind, k, target):
        pltpu.make_async_copy(target.at[k], target.at[k], recv_sem.at[kind, k]).wait()

    wide = SPAN // rows

    def spread(w_ref, data, buffer, k):
        def part(r, carry):
            w = w_ref[pl.ds(pl.multiple_of(r * SPAN, SPAN), SPAN), :]
            value = dot(w, data).astype(jnp.bfloat16)
            buffer[k, pl.ds(r * wide, wide)] = value.reshape(wide, rows, CHUNK)
            return carry

        lax.fori_loop(0, w_ref.shape[0] // SPAN, part, 0)

    def stage_first(k):
        spread(w1_ref, x_ref[:, columns(k)], send_a, k)

    def stage_back(k):
        spread(w4t_ref, cot_ref[:, columns(k)], send_b, k)

    def rows_of(buffer, k, h):
        return buffer[k, :, h * half:(h + 1) * half, :].reshape(owners * half, CHUNK)

    def keep_block(acc, h, r, value):
        which = lax.rem(lax.broadcasted_iota(jnp.int32, (SPAN, 128), 0), half) // 4
        kept = value[:, 0:128]
        for p in range(1, half // 4):
            kept = jnp.where(which == p, value[:, p * 128:(p + 1) * 128], kept)
        acc[h, r * SPAN:(r + 1) * SPAN, :] += kept

    def stage_middle(k):
        arrived(0, k, got_first)
        sent(0, k, send_a)
        size = owners * half
        for h in range(2):
            given = rows_of(got_first, k, h)
            for r in range(size // SPAN):
                at = pl.ds(r * SPAN, SPAN)
                pre = dot(w2_ref[h, at, :], given)
                square = pre * pre
                t = jnp.tanh(ROOT * (pre + CUBIC * (square * pre)))
                cdf = 0.5 * (1.0 + t)
                hidden[h, at, :] = (pre * cdf).astype(jnp.bfloat16)
                slope[h, at, :] = cdf + (0.5 * ROOT) * pre * (1.0 - t * t) * (1.0 + (3.0 * CUBIC) * square)
        each = SPAN // half
        for h in range(2):
            for r in range(size // SPAN):
                value = dot(w3_ref[h, pl.ds(r * SPAN, SPAN), :], hidden[h]).astype(jnp.bfloat16)
                send_a[k, r * each:(r + 1) * each, h * half:(h + 1) * half, :] = value.reshape(each, half, CHUNK)
        post(2, k, send_a, got_mixed)

        arrived(1, k, got_back)
        sent(1, k, send_b)
        for h in range(2):
            given = rows_of(got_back, k, h)
            for r in range(size // SPAN):
                at = pl.ds(r * SPAN, SPAN)
                back = dot(w3t_ref[h, at, :], given)
                back_pre[h, at, :] = (back * slope[h, at, :]).astype(jnp.bfloat16)
        for h in range(2):
            for r in range(size // SPAN):
                value = dot(w2t_ref[h, pl.ds(r * SPAN, SPAN), :], back_pre[h]).astype(jnp.bfloat16)
                send_b[k, r * each:(r + 1) * each, h * half:(h + 1) * half, :] = value.reshape(each, half, CHUNK)
        post(3, k, send_b, got_last)

        for h in range(2):
            for r in range(size // SPAN):
                part = slice(r * each, (r + 1) * each)
                inner = slice(h * half, (h + 1) * half)
                back = got_back[k, part, inner, :].reshape(SPAN, CHUNK)
                keep_block(acc_ld, h, r, dot_nt(back, hidden[h]))
                first = got_first[k, part, inner, :].reshape(SPAN, CHUNK)
                keep_block(acc_lu, h, r, dot_nt(first, back_pre[h]))

    def apply(k, got, w_ref, into_ref):
        everything = got[k].reshape(owners * rows, CHUNK)
        into_ref[:, columns(k)] = dot(w_ref[...], everything).astype(jnp.bfloat16)

    def collect(k, got, data_ref, acc):
        data = data_ref[:, columns(k)]
        odd = lax.rem(lax.broadcasted_iota(jnp.int32, (SPAN, 128), 0), 2) == 1

        def part(r, carry):
            piece = got[k, pl.ds(r * wide, wide)].reshape(SPAN, CHUNK)
            value = dot_nt(piece, data)
            at = pl.ds(pl.multiple_of(r * SPAN, SPAN), SPAN)
            acc[at, :] += jnp.where(odd, value[:, 128:256], value[:, 0:128])
            return carry

        lax.fori_loop(0, owners * rows // SPAN, part, 0)

    def save_out(k):
        return pltpu.make_async_copy(out_ref.at[:, columns(k)], out_hbm.at[:, columns(k)], out_sem.at[0, k])

    def save_gt(k):
        return pltpu.make_async_copy(gt_ref.at[:, columns(k)], gt_hbm.at[:, columns(k)], out_sem.at[1, k])

    def stage_output(k):
        apply(k, got_mixed, w4_ref, out_ref)
        save_out(k).start()

    def stage_grad(k):
        apply(k, got_last, w1t_ref, gt_ref)
        save_gt(k).start()

    def sum_output(k):
        arrived(2, k, got_mixed)
        collect(k, got_mixed, cot_ref, acc_rd)

    def sum_grad(k):
        arrived(3, k, got_last)
        collect(k, got_last, x_ref, acc_ru)

    interleave()
    loads[0].wait()
    stage_first(0)
    loads[1].wait()
    stage_back(0)
    pl.semaphore_wait(barrier, count + 2)
    post(0, 0, send_a, got_first)
    post(1, 0, send_b, got_back)
    loads[2].wait()
    loads[3].wait()

    def ahead(k):
        stage_first(k)
        post(0, k, send_a, got_first)
        stage_back(k)
        post(1, k, send_b, got_back)

    for k in range(1, AHEAD):
        ahead(k)
    for acc in (acc_ru, acc_rd, acc_ld, acc_lu):
        acc[...] = jnp.zeros_like(acc)
    loads[4].wait()
    loads[5].wait()
    expand()
    turned()

    def step(k, carry):
        stage_middle(k)

        @pl.when(k + AHEAD < chunks)
        def _():
            ahead(k + AHEAD)

        @pl.when(k >= LAG)
        def _():
            sum_output(k - LAG)
            stage_output(k - LAG)
            sum_grad(k - LAG)
            stage_grad(k - LAG)

        return carry

    lax.fori_loop(0, chunks, step, 0)

    part = grads.shape[1] // 2
    core = lax.rem(tok, 2)
    mine = pl.ds(pl.multiple_of(core * part, part), part)
    theirs = pl.ds(pl.multiple_of(part - core * part, part), part)

    def pair(i):
        return pltpu.make_async_remote_copy(
            src_ref=grads.at[i, theirs], dst_ref=near.at[i], send_sem=sum_send.at[0, i], recv_sem=sum_recv.at[0, i],
            device_id=(core_peer, me), device_id_type=MESH,
        )

    def across(i):
        return pltpu.make_async_remote_copy(
            src_ref=own.at[i], dst_ref=far.at[i], send_sem=sum_send.at[1, i], recv_sem=sum_recv.at[1, i],
            device_id=(far_peer, me), device_id_type=MESH,
        )

    def share(i):
        return pltpu.make_async_remote_copy(
            src_ref=sums_ref.at[i], dst_ref=sums_hbm.at[i, mine],
            send_sem=sum_send.at[2, i], recv_sem=sum_recv.at[2, i],
            device_id=(core_peer, me), device_id_type=MESH,
        )

    def save(i):
        return pltpu.make_async_copy(sums_ref.at[i], sums_hbm.at[i, mine], save_sem.at[i])

    def begin(i):
        pair(i).start()

    def middle(i):
        pair(i).wait()
        own[i] = (grads[i, mine, :] + near[i]).astype(jnp.bfloat16)
        across(i).start()

    def finish(i):
        across(i).wait()
        sums_ref[i] = own[i].astype(jnp.float32) + far[i].astype(jnp.float32)
        share(i).start()
        save(i).start()

    lane = lax.broadcasted_iota(jnp.int32, (owners, 128), 1)
    for h in range(2):
        for c in range(half // 2):
            for s in range(2):
                ld = acc_ld[h, pl.ds(2 * c + s, owners, stride=half), :]
                lu = acc_lu[h, pl.ds(2 * c + s, owners, stride=half), :]
                if c % 2 == 0:
                    both = jnp.where(lane < 64, ld, pltpu.roll(lu, 64, 1))
                else:
                    both = jnp.where(lane < 64, pltpu.roll(ld, 64, 1), lu)
                base = (h * (half // 2) + c) * 2 * owners
                grads[0, pl.ds(base + s, owners, stride=2), :] = both
    begin(0)

    size = owners * half
    last = chunks - 1
    for k in range(chunks - LAG, last):
        sum_output(k)
        stage_output(k)
        sum_grad(k)
        stage_grad(k)
    sum_output(last)
    for s in range(2):
        grads[1, s * size:(s + 1) * size, :] = acc_rd[pl.ds(s, size, stride=2), :]
    begin(1)
    middle(0)
    stage_output(last)
    middle(1)
    sum_grad(last)
    for s in range(2):
        grads[2, s * size:(s + 1) * size, :] = acc_ru[pl.ds(s, size, stride=2), :]
    begin(2)
    stage_grad(last)
    middle(2)
    finish(0)
    finish(1)
    finish(2)

    def drain(k, carry):
        sent(2, k, send_a)
        sent(3, k, send_b)
        save_out(k).wait()
        save_gt(k).wait()
        return carry

    lax.fori_loop(0, chunks, drain, 0)
    for i in range(3):
        share(i).wait()
        save(i).wait()


def finish(
    factor, out_hbm, gt_hbm, sums_hbm, out_to, gt_to, ru_to, lu_to, ld_to, rd_to,
    held, sums_ref, ru_ref, lu_ref, ld_ref, rd_ref, sem, sum_sem, turn_sem,
):
    slabs = held.shape[1]
    deep = out_hbm.shape[0] // slabs
    enter, leave = [], []
    sums = [pltpu.make_async_copy(sums_hbm.at[i], sums_ref.at[i], sum_sem.at[i]) for i in range(3)]
    for p in range(slabs):
        at = pl.ds(p * deep, deep)
        for i, (source, target) in enumerate(((out_hbm, out_to), (gt_hbm, gt_to))):
            enter.append(pltpu.make_async_copy(source.at[at], held.at[i, p], sem.at[0, i, p]))
            leave.append(pltpu.make_async_copy(held.at[i, p], target.at[at], sem.at[1, i, p]))
    for copy in enter[:2] + sums + enter[2:]:
        copy.start()
    turned = [
        pltpu.make_async_copy(source, target, turn_sem.at[i])
        for i, (source, target) in enumerate(((ld_ref, ld_to), (lu_ref, lu_to), (rd_ref, rd_to), (ru_ref, ru_to)))
    ]

    def forward(part):
        for i in part:
            enter[i].wait()
            leave[i].start()

    units = ld_ref.shape[1]
    size = sums_ref.shape[1] // 2
    forward(range(0, 2))
    sums[0].wait()
    for c in range(ld_ref.shape[0]):
        both = sums_ref[0, c * units:(c + 1) * units, :] * factor
        ld_ref[c] = both[:, :units]
        lu_ref[c] = both.T[units:, :]
    turned[0].start()
    turned[1].start()
    forward(range(2, 4))
    sums[1].wait()
    for s in range(2):
        rd_ref[s] = (sums_ref[1, s * size:(s + 1) * size, :] * factor).T
    turned[2].start()
    forward(range(4, 6))
    sums[2].wait()
    for s in range(2):
        ru_ref[s] = sums_ref[2, s * size:(s + 1) * size, :] * factor
    turned[3].start()
    forward(range(6, 2 * slabs))
    for copy in leave + turned:
        copy.wait()


def shards(tokens, cotangent, right_up, left_up, left_down, right_down):
    tok_count = lax.axis_size("tok")
    owners = lax.axis_size("blk")
    factor = float(tokens.shape[2] * tok_count) ** (-0.5)
    pair, width, count = tokens.shape
    hidden_blocks = right_up.shape[1]
    own_blocks = left_up.shape[0]
    units = left_up.shape[1]
    eight = own_blocks // 2
    chunks = count // CHUNK
    bf = jnp.bfloat16

    wide, deep = pair * hidden_blocks, pair * width
    size = eight * units
    rows = pair * own_blocks
    flow = pltpu.VMEM((chunks, owners, rows, CHUNK), bf)
    vmem = pl.BlockSpec(memory_space=pltpu.VMEM)
    hbm = pl.BlockSpec(memory_space=pltpu.HBM)
    output, grad_tokens, sums = pl.pallas_call(
        functools.partial(kernel, chunks, owners),
        out_shape=(
            jax.ShapeDtypeStruct((deep, count), bf),
            jax.ShapeDtypeStruct((deep, count), bf),
            jax.ShapeDtypeStruct((3, wide, 128), jnp.float32),
        ),
        in_specs=[hbm, hbm, vmem, vmem, hbm, hbm],
        out_specs=(hbm, hbm, hbm),
        scratch_shapes=[
            pltpu.VMEM((deep, count), bf), pltpu.VMEM((deep, count), bf),
            pltpu.VMEM(left_up.shape, bf), pltpu.VMEM(left_down.shape, bf),
            pltpu.VMEM((deep, count), bf), pltpu.VMEM((deep, count), bf),
            pltpu.VMEM((wide, deep), bf), pltpu.VMEM((deep, wide), bf),
            pltpu.VMEM((2, size, size), bf), pltpu.VMEM((2, size, size), bf),
            pltpu.VMEM((2, size, size), bf), pltpu.VMEM((2, size, size), bf),
            pltpu.VMEM((deep, wide), bf), pltpu.VMEM((wide, deep), bf),
            flow, flow, flow, flow, flow, flow,
            pltpu.VMEM((2, size, CHUNK), bf),
            pltpu.VMEM((2, size, CHUNK), jnp.float32),
            pltpu.VMEM((2, size, CHUNK), bf),
            pltpu.VMEM((wide, 128), jnp.float32),
            pltpu.VMEM((wide, 128), jnp.float32),
            pltpu.VMEM((2, size, 128), jnp.float32),
            pltpu.VMEM((2, size, 128), jnp.float32),
            pltpu.VMEM((3, wide, 128), jnp.float32),
            pltpu.VMEM((3, wide // 2, 128), jnp.float32),
            pltpu.VMEM((3, wide // 2, 128), bf),
            pltpu.VMEM((3, wide // 2, 128), bf),
            pltpu.VMEM((3, wide // 2, 128), jnp.float32),
            pltpu.SemaphoreType.DMA((4, chunks)),
            pltpu.SemaphoreType.DMA((4, chunks)),
            pltpu.SemaphoreType.DMA((3, 3)),
            pltpu.SemaphoreType.DMA((3, 3)),
            pltpu.SemaphoreType.DMA((6,)),
            pltpu.SemaphoreType.DMA((2, chunks)),
            pltpu.SemaphoreType.DMA((3,)),
        ],
        compiler_params=pltpu.CompilerParams(
            collective_id=0, has_side_effects=True, vmem_limit_bytes=60 << 20
        ),
        name="monarch",
    )(
        tokens.reshape(deep, count), cotangent.reshape(deep, count),
        right_up, right_down, left_up, left_down,
    )
    shape = tokens.shape
    output, grad_tokens, grad_ru, grad_lu, grad_ld, grad_rd = pl.pallas_call(
        functools.partial(finish, factor),
        out_shape=(
            jax.ShapeDtypeStruct((deep, count), bf),
            jax.ShapeDtypeStruct((deep, count), bf),
            jax.ShapeDtypeStruct(right_up.shape, jnp.float32),
            jax.ShapeDtypeStruct(left_up.shape, jnp.float32),
            jax.ShapeDtypeStruct(left_down.shape, jnp.float32),
            jax.ShapeDtypeStruct(right_down.shape, jnp.float32),
        ),
        in_specs=[hbm, hbm, hbm],
        out_specs=(hbm,) * 6,
        scratch_shapes=[
            pltpu.VMEM((2, 4, deep // 4, count), bf),
            pltpu.VMEM((3, wide, 128), jnp.float32),
            pltpu.VMEM(right_up.shape, jnp.float32), pltpu.VMEM(left_up.shape, jnp.float32),
            pltpu.VMEM(left_down.shape, jnp.float32), pltpu.VMEM(right_down.shape, jnp.float32),
            pltpu.SemaphoreType.DMA((2, 2, 4)), pltpu.SemaphoreType.DMA((3,)), pltpu.SemaphoreType.DMA((4,)),
        ],
        compiler_params=pltpu.CompilerParams(vmem_limit_bytes=60 << 20),
        name="finish",
    )(output, grad_tokens, sums)
    return (output.reshape(shape), grad_tokens.reshape(shape), grad_ru, grad_lu, grad_ld, grad_rd)


def solution(mesh):
    split = P("blk", None, "tok")
    whole = P("blk", None, None)
    return jax.shard_map(
        shards,
        mesh=mesh,
        in_specs=(split, split, whole, whole, whole, whole),
        out_specs=(split, split, whole, whole, whole, whole),
        check_vma=False,
    )
```
